128 devices in a mesh: row: 16 (over z, y), col: 8 (over x, core).
Axes of the slice: x: 4, y: 4, z: 4, core: 2. Of those that a mesh axis runs over, the one named last changes fastest.
Arguments:
- features: float32 [65536, 512], P(('row', 'col')), may hold values from -6 to 6
- tiles: float32 [16, 8, 128, 128, 128], P('row', 'col'), may hold values from -0.4 to 0.4
- tile_rows: int32 [16, 8, 128], P('row', 'col'), may hold values from 0 to 31
- tile_cols: int32 [16, 8, 128], P('row', 'col'), may hold values from 0 to 31
- tile_count: int32 [16, 8], P('row', 'col'), may hold values from 16 to 128, as said below
- needed: int32 [16, 8, 16, 2], P('row', 'col'), may hold values from 0 to 3, as said below
- w_in: bfloat16 [512, 2048], replicated, may hold values from -0.25 to 0.25
- bias_in: float32 [2048], replicated, may hold values from -5 to 5
- w_out: bfloat16 [2048, 512], replicated, may hold values from -0.125 to 0.125
- bias_out: float32 [512], replicated, may hold values from -5 to 5
Outputs:
- updated: bfloat16 [65536, 512], P(('row', 'col'))
The draws below stay inside these ranges and needn't reach their ends.
Inputs may be any that keep to these rules, and one draw needn't show every extreme that they name: tile_count of every grid cell lies between 16 and 64, except one cell of each draw that has all 128 tiles live. Each list needed[r, c, q] holds 2 different block numbers.
All inputs are finite; a program needn't handle non-finite values.
Results may differ from the reference program's by a relative error of at most 0.0054.
Values sent between devices are 32-bit elements; how exact they have to be, the bound alone decides.
No kernel may reach another device: no remote copies, remote signals or barrier semaphores. Data moves between devices by JAX's collectives and lax.ppermute only.
A program may use at most 128 MiB of HBM per device.

```python
import jax
import jax.numpy as jnp
from jax import lax

F = 512
HID = 2048
TILE = 128
BPS = 4
TPD = 128
MAXB = 2
GRID_R = 16
GRID_C = 8
NODES = 65536


def draw_needed(key, part):
    scores = jax.random.randint(jax.random.fold_in(key, 11), (GRID_R, GRID_C, GRID_R, BPS), 0, 1 << 20)
    scores = scores * BPS + jnp.arange(BPS, dtype=jnp.int32)
    order = jnp.argsort(scores, axis=-1)
    return order[..., :MAXB].astype(jnp.int32)


def draw_tile_count(key, part):
    first = jax.random.fold_in(key, 23)
    second = jax.random.fold_in(key, 29)
    base = jax.random.randint(first, (GRID_R * GRID_C,), TPD // 8, TPD // 2 + 1)
    chosen = jax.random.randint(second, (), 0, GRID_R * GRID_C)
    filled = jnp.where(jnp.arange(GRID_R * GRID_C) == chosen, TPD, base)
    return filled.reshape(GRID_R, GRID_C).astype(jnp.int32)


def place_ends(entries, stream_key, smallest, top_value):
    longest = entries.shape.index(max(entries.shape))
    spots = []
    for shift in (0, 1):
        where = [jax.random.randint(jax.random.fold_in(stream_key, axis), (), 0, length) for axis, length in enumerate(entries.shape)]
        where[longest] = (where[longest] + shift) % entries.shape[longest]
        spots.append(tuple(where))
    return entries.at[spots[0]].set(smallest).at[spots[1]].set(top_value)


def levels(own_key, shape, split, least, largest):
    def one(axis_at, blocks):
        heights = jax.random.uniform(jax.random.fold_in(jax.random.fold_in(own_key, 6), axis_at), (blocks,), jnp.float32, least / len(split), largest / len(split))
        return jnp.repeat(jnp.exp(heights), shape[axis_at] // blocks).reshape((-1,) + (1,) * (len(shape) - axis_at - 1))

    factor_of = one(*split[0])
    for cut in split[1:]:
        factor_of = factor_of * one(*cut)
    return factor_of


def bell_draw(rng, dims, scale, bound, pieces=(), held_as=jnp.bfloat16):
    drawn = scale * jax.random.normal(rng, dims, jnp.float32)
    if pieces:
        drawn = drawn * levels(rng, dims, pieces, -0.22, 0.18)
    return jnp.clip(drawn, -bound, bound).astype(held_as)


def setup_inputs(seed: int = 0) -> dict:
    arg_keys = jax.random.split(jax.random.key(seed), 11)
    features = bell_draw(arg_keys[0], (NODES, F), 1.0, 6.0, ((0, 128),), jnp.float32)
    tiles = bell_draw(arg_keys[1], (GRID_R, GRID_C, TPD, TILE, TILE), 0.05, 0.4, ((0, 16), (1, 8)), jnp.float32)
    tile_rows = place_ends(jax.random.randint(arg_keys[2], (GRID_R, GRID_C, TPD), 0, GRID_C * BPS), jax.random.fold_in(arg_keys[2], 1), 0, (GRID_C * BPS) - 1).astype(jnp.int32)
    tile_cols = place_ends(jax.random.randint(arg_keys[3], (GRID_R, GRID_C, TPD), 0, GRID_R * MAXB), jax.random.fold_in(arg_keys[3], 1), 0, (GRID_R * MAXB) - 1).astype(jnp.int32)
    tile_count = draw_tile_count(jax.random.fold_in(arg_keys[10], 71), 0)
    needed = draw_needed(jax.random.fold_in(arg_keys[10], 71), 0)
    w_in = bell_draw(arg_keys[6], (F, HID), F ** -0.5, 0.25)
    bias_in = bell_draw(arg_keys[7], (HID,), 1.0, 5.0, (), jnp.float32)
    w_out = bell_draw(arg_keys[8], (HID, F), HID ** -0.5, 0.125)
    bias_out = bell_draw(arg_keys[9], (F,), 1.0, 5.0, (), jnp.float32)
    return {"features": features, "tiles": tiles, "tile_rows": tile_rows, "tile_cols": tile_cols, "tile_count": tile_count, "needed": needed, "w_in": w_in, "bias_in": bias_in, "w_out": w_out, "bias_out": bias_out}


def reference(features, tiles, tile_rows, tile_cols, tile_count, needed, w_in, bias_in, w_out, bias_out):
    blocks = features.reshape(-1, TILE, F)
    row_blocks = GRID_C * BPS

    def cell(total, position):
        grid_row = position // GRID_C
        grid_col = position % GRID_C
        column_slot = tile_cols[grid_row, grid_col]
        source = column_slot // MAXB
        local = needed[grid_row, grid_col].reshape(-1)[column_slot]
        source_block = ((source * GRID_C + grid_col) * BPS + local).astype(jnp.int32)
        target_block = (grid_row * row_blocks + tile_rows[grid_row, grid_col]).astype(jnp.int32)
        live = (jnp.arange(TPD) < tile_count[grid_row, grid_col]).astype(jnp.float32)
        inputs = blocks[source_block]
        product = jnp.einsum("tpq,tqf->tpf", tiles[grid_row, grid_col], inputs, precision=lax.Precision.HIGHEST)
        product = product * live[:, None, None]
        return total.at[target_block].add(product), None

    aggregate, _ = lax.scan(cell, jnp.zeros(blocks.shape, jnp.float32), jnp.arange(GRID_R * GRID_C, dtype=jnp.int32))
    aggregate = aggregate.reshape(features.shape)
    mixed = (1.25 * features + aggregate).astype(jnp.bfloat16)
    hidden = jax.nn.relu(jnp.dot(mixed, w_in, preferred_element_type=jnp.float32) + bias_in).astype(jnp.bfloat16)
    return (jnp.dot(hidden, w_out, preferred_element_type=jnp.float32) + bias_out).astype(jnp.bfloat16)
```

```python
import jax
import jax.numpy as jnp
from jax import lax
from jax.experimental import pallas as pl
from jax.experimental.pallas import tpu as pltpu
from jax.sharding import PartitionSpec as P

gin_epsilon = 0.25
unroll = 4
span = 256


def add_tiles(count_ref, row_ref, pos_ref, tile_ref, pool_ref, out_ref):
    out_ref[...] = jnp.zeros_like(out_ref)
    count = count_ref[0]

    def turn(step, carry):
        products = []
        for lane in range(unroll):
            slot = step * unroll + lane
            source = pool_ref[pos_ref[slot]].astype(jnp.bfloat16)
            product = jnp.dot(tile_ref[slot], source, preferred_element_type=jnp.float32)
            live = (slot < count).astype(jnp.float32)
            products.append((row_ref[slot], product * live))
        for target, product in products:
            out_ref[target] += product
        return carry

    lax.fori_loop(0, (count + unroll - 1) // unroll, turn, 0)


def aggregate(count, row, pos, tiles, pool, row_blocks):
    tile_total, edge, _ = tiles.shape
    pool_blocks, _, width = pool.shape
    return pl.pallas_call(
        add_tiles,
        grid_spec=pltpu.PrefetchScalarGridSpec(
            num_scalar_prefetch=3,
            grid=(width // span,),
            in_specs=[
                pl.BlockSpec((tile_total, edge, edge), lambda i, *_: (0, 0, 0)),
                pl.BlockSpec((pool_blocks, edge, span), lambda i, *_: (0, 0, i)),
            ],
            out_specs=pl.BlockSpec((row_blocks, edge, span), lambda i, *_: (0, 0, i)),
        ),
        out_shape=jax.ShapeDtypeStruct((row_blocks, edge, width), jnp.float32),
        compiler_params=pltpu.CompilerParams(vmem_limit_bytes=56 << 20),
    )(count, row, pos, tiles, pool)


def on_device(
    features, tiles, tile_rows, tile_cols, tile_count, needed, w_in, bias_in, w_out, bias_out
):
    tile_edge = tiles.shape[-1]
    width = features.shape[1]
    blocks_dev = features.shape[0] // tile_edge
    grid_cols = lax.axis_size("col")
    slot_count = needed.shape[-1]
    row_blocks = grid_cols * blocks_dev
    own_blocks = features.reshape(blocks_dev, tile_edge, width)
    tile_col = tile_cols[0, 0]
    column_pool = lax.all_gather(own_blocks, "row", axis=0, tiled=True)
    position = tile_col // slot_count * blocks_dev + jnp.take(needed[0, 0].reshape(-1), tile_col)
    partial_value = aggregate(
        tile_count[0],
        tile_rows[0, 0],
        position,
        tiles[0, 0].astype(jnp.bfloat16),
        column_pool,
        row_blocks,
    )
    summed = lax.psum_scatter(
        partial_value.reshape(row_blocks * tile_edge, width), "col", scatter_dimension=0, tiled=True
    )
    mixed = ((1.0 + gin_epsilon) * features + summed).astype(jnp.bfloat16)
    hidden = jax.nn.relu(jnp.dot(mixed, w_in, preferred_element_type=jnp.float32) + bias_in).astype(
        jnp.bfloat16
    )
    return (jnp.dot(hidden, w_out, preferred_element_type=jnp.float32) + bias_out).astype(
        jnp.bfloat16
    )


def solution(mesh):
    placed = (
        P(("row", "col"), None),
        P("row", "col", None, None, None),
        P("row", "col", None),
        P("row", "col", None),
        P("row", "col"),
        P("row", "col", None, None),
        P(),
        P(),
        P(),
        P(),
    )
    return jax.shard_map(
        on_device, mesh=mesh, in_specs=placed, out_specs=P(("row", "col"), None), check_vma=False
    )
```

```python
import jax
import jax.numpy as jnp
from jax import lax
from jax.experimental import pallas as pl
from jax.experimental.pallas import tpu as pltpu
from jax.sharding import PartitionSpec as P


gin_epsilon = 0.25
unroll = 8
span = 256
side = 4
cores = 2
picks = 2
note_rows = 8
lanes = 128
chunk = 512

in_vmem = pl.BlockSpec(memory_space=pltpu.VMEM)
in_smem = pl.BlockSpec(memory_space=pltpu.SMEM)


def row_shift(step_z, step_y):
    return [
        (z * side + y, (z + step_z) % side * side + (y + step_y) % side)
        for z in range(side)
        for y in range(side)
    ]


def col_shift(step_x, step_core):
    return [
        (x * cores + k, (x + step_x) % side * cores + (k + step_core) % cores)
        for x in range(side)
        for k in range(cores)
    ]


def from_z(value, step):
    return lax.ppermute(value, "row", row_shift(-step, 0))


def from_y(value, step):
    return lax.ppermute(value, "row", row_shift(0, -step))


def back(step):
    return (side - step) % side


def half_at(number, half):
    return pl.ds(pl.multiple_of(number * half, half), half)


def spot_of(d, j, half):
    return slice((d * picks + j) * half, (d * picks + j + 1) * half)


def split(feature_ref, need_ref, *outs):
    half = lanes // 2
    rows = feature_ref.shape[0] // 2
    need = need_ref[...].astype(jnp.float32)
    for group in range(len(outs) // 2):
        part = slice(group * span, (group + 1) * span)
        for place, out in enumerate(outs[2 * group : 2 * group + 2]):
            for block in range(rows // half):
                start = (2 * block + place) * half
                out[block * half : (block + 1) * half, :] = feature_ref[start : start + half, part]
            if group == 0:
                out[rows:, :] = jnp.zeros((note_rows, span), jnp.float32)
                out[rows : rows + need.shape[0], : need.shape[1]] = need


def plan(row_ref, col_ref, count_ref, plan_ref, blocks_dev, entries):
    my_z = lax.axis_index("row") // side
    my_y = lax.axis_index("row") % side
    my_x = lax.axis_index("col") // cores
    my_core = lax.axis_index("col") % cores

    def write(at, slot, row, pos):
        plan_ref[at] = slot
        plan_ref[at + entries] = row
        plan_ref[at + 2 * entries] = pos

    def turn(slot, ends):
        target = row_ref[slot]
        column = target // blocks_dev
        row = lax.rem(column // cores - my_x + side, side) * blocks_dev + target % blocks_dev
        other = (column % cores != my_core).astype(jnp.int32)
        owner = col_ref[slot] // picks
        away_z = lax.rem(owner // side - my_z + side, side)
        away_y = lax.rem(owner % side - my_y + side, side)
        pos = (away_z * side + away_y) * picks + col_ref[slot] % picks
        for which, end in enumerate(ends):
            write(which * 3 * entries + end, slot, row, pos)
        return ends[0] + other, ends[1] + 1 - other

    ends = lax.fori_loop(0, count_ref[0, 0], turn, (0, 0))
    for which, end in enumerate(ends):
        plan_ref[6 * entries + which] = end
        for extra in range(unroll):
            write(which * 3 * entries + end + extra, 0, 0, 0)


def pack(half, *refs):
    first, second = refs[:side], refs[side : 2 * side]
    notes_from = refs[2 * side : 4 * side - 2]
    outs = refs[4 * side - 2 : 6 * side - 4]
    notes, sems = refs[6 * side - 4 :]
    rows = side * half
    copies = [
        pltpu.make_async_copy(
            source.at[rows : rows + note_rows, :lanes], notes.at[at], sems.at[at]
        )
        for at, source in enumerate(notes_from)
    ]
    for copy in copies:
        copy.start()
    for copy in copies:
        copy.wait()
    my_z = lax.axis_index("row") // side
    my_y = lax.axis_index("row") % side
    for away in range(1, side):
        for d in range(side):
            next_y = lax.rem(my_y + d, side)
            next_z = lax.rem(my_z + d, side)
            for j in range(picks):
                spot = spot_of(d, j, half)
                along_z = notes[away - 1, j, my_z * side + next_y].astype(jnp.int32)
                outs[away - 1][spot, :] = first[d][half_at(along_z, half), :]
                along_y = notes[side + away - 2, j, next_z * side + my_y].astype(jnp.int32)
                outs[side + away - 2][spot, :] = second[d][half_at(along_y, half), :]


def pack_group(first, second, notes, half):
    packed = jax.ShapeDtypeStruct((side * picks * half, span), jnp.float32)
    number = 2 * (side - 1)
    return pl.pallas_call(
        lambda *refs: pack(half, *refs),
        in_specs=[in_vmem] * (2 * side + number),
        out_specs=[in_vmem] * number,
        scratch_shapes=[
            pltpu.SMEM((number, note_rows, lanes), jnp.float32),
            pltpu.SemaphoreType.DMA((number,)),
        ],
        out_shape=[packed] * number,
        compiler_params=pltpu.CompilerParams(vmem_limit_bytes=16 << 20),
        cost_estimate=pl.CostEstimate(flops=0, bytes_accessed=5 << 20, transcendentals=0),
        name="pack",
    )(*first, *second, *notes)


def add_tiles(which, plan_ref, tile_ref, pool, total):
    entries = tile_ref.shape[0] + unroll
    base = which * 3 * entries
    total[...] = jnp.zeros_like(total)
    count = plan_ref[6 * entries + which]

    def turn(step, carry):
        products = []
        for lane in range(unroll):
            at = base + step * unroll + lane
            product = jnp.dot(
                tile_ref[plan_ref[at]],
                pool[plan_ref[at + 2 * entries]],
                preferred_element_type=jnp.float32,
            )
            live = (step * unroll + lane < count).astype(jnp.float32)
            products.append((plan_ref[at + entries], product * live))
        for target, product in products:
            total[target] += product
        return carry

    lax.fori_loop(0, (count + unroll - 1) // unroll, turn, 0)


def combine(plan_ref, need_ref, tile_ref, *refs):
    first, second = refs[:side], refs[side : 2 * side]
    along_z = refs[2 * side : 3 * side - 1]
    along_y = refs[3 * side - 1 : 4 * side - 2]
    total, pool = refs[4 * side - 2 :]
    half = pool.shape[1] // 2
    top, low = slice(0, half), slice(half, 2 * half)
    my_z = lax.axis_index("row") // side
    my_y = lax.axis_index("row") % side
    for d in range(side):
        next_y = lax.rem(my_y + d, side)
        next_z = lax.rem(my_z + d, side)
        for j in range(picks):
            mine = need_ref[j, my_z * side + next_y]
            pool[d * picks + j, top, :] = first[d][half_at(mine, half), :].astype(pool.dtype)
            mine = need_ref[j, next_z * side + my_y]
            pool[d * side * picks + j, low, :] = second[d][half_at(mine, half), :].astype(
                pool.dtype
            )
            spot = spot_of(d, j, half)
            for away in range(1, side):
                pool[(back(away) * side + d) * picks + j, top, :] = along_z[away - 1][
                    spot, :
                ].astype(pool.dtype)
                pool[(d * side + back(away)) * picks + j, low, :] = along_y[away - 1][
                    spot, :
                ].astype(pool.dtype)
    add_tiles(0, plan_ref, tile_ref, pool, total)


def combine_sent(listed, need, tiles, first, second, along_z, along_y, blocks):
    edge = tiles.shape[1]
    return pl.pallas_call(
        combine,
        in_specs=[in_smem] * 2 + [in_vmem] * (4 * side - 1),
        out_specs=[in_vmem] * 2,
        out_shape=[
            jax.ShapeDtypeStruct((blocks, edge, span), jnp.float32),
            jax.ShapeDtypeStruct((side * side * picks, edge, span), jnp.bfloat16),
        ],
        compiler_params=pltpu.CompilerParams(vmem_limit_bytes=24 << 20),
        cost_estimate=pl.CostEstimate(flops=2 << 30, bytes_accessed=10 << 20, transcendentals=0),
        name="combine",
    )(listed, need, tiles, *first, *second, *along_z, *along_y)


def combine_kept(listed, tiles, pool, blocks):
    edge = tiles.shape[1]
    return pl.pallas_call(
        lambda plan_ref, tile_ref, pool, total: add_tiles(1, plan_ref, tile_ref, pool, total),
        in_specs=[in_smem] + [in_vmem] * 2,
        out_specs=in_vmem,
        out_shape=jax.ShapeDtypeStruct((blocks, edge, span), jnp.float32),
        compiler_params=pltpu.CompilerParams(vmem_limit_bytes=24 << 20),
        cost_estimate=pl.CostEstimate(flops=2 << 30, bytes_accessed=8 << 20, transcendentals=0),
        name="keep",
    )(listed, tiles, pool)


def mixed_of(group, feature_ref, totals):
    part = slice(group * span, (group + 1) * span)
    summed = totals[0][...]
    for other in totals[1:]:
        summed = summed + other[...]
    return ((1.0 + gin_epsilon) * feature_ref[:, part] + summed).astype(jnp.bfloat16)


def begin_mlp(feature_ref, w_ref, bias_ref, *refs):
    totals, out_ref, mixed = refs[:side], refs[side], refs[side + 1]
    mixed[...] = mixed_of(0, feature_ref, totals)

    def turn(step, carry):
        part = pl.ds(pl.multiple_of(step * chunk, chunk), chunk)
        out_ref[:, part] = (
            jnp.dot(mixed[...], w_ref[:span, part], preferred_element_type=jnp.float32)
            + bias_ref[:, part]
        )
        return carry

    lax.fori_loop(0, w_ref.shape[1] // chunk, turn, 0)


def end_mlp(feature_ref, w_ref, before_ref, w_out_ref, bias_ref, *refs):
    totals, out_ref, mixed, total = refs[:side], refs[side], refs[side + 1], refs[side + 2]
    mixed[...] = mixed_of(1, feature_ref, totals)
    total[...] = jnp.broadcast_to(bias_ref[...], total.shape)

    def turn(step, carry):
        part = pl.ds(pl.multiple_of(step * chunk, chunk), chunk)
        hidden = before_ref[:, part] + jnp.dot(
            mixed[...], w_ref[span:, part], preferred_element_type=jnp.float32
        )
        hidden = jnp.maximum(hidden, 0.0).astype(jnp.bfloat16)
        total[...] += jnp.dot(hidden, w_out_ref[part, :], preferred_element_type=jnp.float32)
        return carry

    lax.fori_loop(0, w_ref.shape[1] // chunk, turn, 0)
    out_ref[...] = total[...].astype(out_ref.dtype)


def on_device(
    features, tiles, tile_rows, tile_cols, tile_count, needed, w_in, bias_in, w_out, bias_out
):
    tile_total, edge = tiles.shape[2], tiles.shape[-1]
    half = edge // 2
    nodes, width = features.shape
    blocks_dev = nodes // edge
    hidden_size = w_in.shape[1]
    blocks = side * blocks_dev
    groups = width // span
    rows = nodes // 2

    need = needed[0, 0].T
    payload = [
        jax.ShapeDtypeStruct((rows + (note_rows if group == 0 else 0), span), jnp.float32)
        for group in range(groups)
        for _ in range(2)
    ]
    own = pl.pallas_call(
        split,
        in_specs=[in_vmem] * 2,
        out_specs=[in_vmem] * len(payload),
        out_shape=payload,
        compiler_params=pltpu.CompilerParams(vmem_limit_bytes=8 << 20),
        cost_estimate=pl.CostEstimate(flops=0, bytes_accessed=2 << 20, transcendentals=0),
        name="split",
    )(features, need)
    firsts, seconds = [], []
    for group in range(groups):
        first = [own[2 * group]] + [None] * (side - 1)
        second = [own[2 * group + 1]] + [None] * (side - 1)
        for away in (1, 3, 2):
            first[away] = from_y(first[0], away)
            second[away] = from_z(second[0], away)
        firsts.append(first)
        seconds.append(second)
    notes = seconds[0][1:] + firsts[0][1:]

    entries = tile_total + unroll
    listed = pl.pallas_call(
        lambda *refs: plan(*refs, blocks_dev, entries),
        in_specs=[in_smem] * 3,
        out_specs=in_smem,
        out_shape=jax.ShapeDtypeStruct((1024,), jnp.int32),
        cost_estimate=pl.CostEstimate(flops=0, bytes_accessed=1 << 20, transcendentals=0),
        name="plan",
    )(tile_rows[0, 0], tile_cols[0, 0], tile_count)
    tiles_low = tiles[0, 0].astype(jnp.bfloat16)

    sums = []
    for group in range(groups):
        first, second = firsts[group], seconds[group]
        packed = pack_group(first, second, notes, half)
        along_z, along_y = [None] * (side - 1), [None] * (side - 1)
        for away in (1, 3, 2):
            along_z[away - 1] = from_z(packed[away - 1], -away)
            along_y[away - 1] = from_y(packed[side + away - 2], -away)
        send, pool = combine_sent(listed, need, tiles_low, first, second, along_z, along_y, blocks)
        arrived = lax.ppermute(send, "col", col_shift(0, 1))
        keep = combine_kept(listed, tiles_low, pool, blocks)
        parts = [
            (
                keep[k * blocks_dev : (k + 1) * blocks_dev]
                + arrived[k * blocks_dev : (k + 1) * blocks_dev]
            ).reshape(nodes, span)
            for k in range(side)
        ]
        total = [parts[0]]
        for k in (1, 3, 2):
            total.append(lax.ppermute(parts[k], "col", col_shift(k, 0)))
        sums.append(total)

    before = pl.pallas_call(
        begin_mlp,
        in_specs=[in_vmem] * (3 + side),
        out_specs=in_vmem,
        out_shape=jax.ShapeDtypeStruct((nodes, hidden_size), jnp.float32),
        scratch_shapes=[pltpu.VMEM((nodes, span), jnp.bfloat16)],
        compiler_params=pltpu.CompilerParams(vmem_limit_bytes=24 << 20),
        cost_estimate=pl.CostEstimate(
            flops=1 << 29, bytes_accessed=8 << 20, transcendentals=0
        ),
        name="begin",
    )(features, w_in, bias_in.reshape(1, -1), *sums[0])
    return pl.pallas_call(
        end_mlp,
        in_specs=[in_vmem] * (5 + side),
        out_specs=in_vmem,
        out_shape=jax.ShapeDtypeStruct((nodes, width), jnp.bfloat16),
        scratch_shapes=[
            pltpu.VMEM((nodes, span), jnp.bfloat16),
            pltpu.VMEM((nodes, width), jnp.float32),
        ],
        compiler_params=pltpu.CompilerParams(vmem_limit_bytes=24 << 20),
        cost_estimate=pl.CostEstimate(
            flops=3 << 29, bytes_accessed=8 << 20, transcendentals=0
        ),
        name="end",
    )(features, w_in, before, w_out, bias_out.reshape(1, -1), *sums[1])


def solution(mesh):
    placed = (
        P(("row", "col"), None),
        P("row", "col", None, None, None),
        P("row", "col", None),
        P("row", "col", None),
        P("row", "col"),
        P("row", "col", None, None),
        P(),
        P(),
        P(),
        P(),
    )

    return jax.shard_map(
        on_device, mesh=mesh, in_specs=placed, out_specs=P(("row", "col"), None), check_vma=False
    )
```

```python
import jax
import jax.numpy as jnp
from jax import lax
from jax.experimental import pallas as pl
from jax.experimental.pallas import tpu as pltpu
from jax.sharding import PartitionSpec as P


gin_epsilon = 0.25
unroll = 8
span = 256
side = 4
cores = 2
picks = 2
parts = 3
note_rows = 8
lanes = 128
chunk = 512

in_vmem = pl.BlockSpec(memory_space=pltpu.VMEM)
in_smem = pl.BlockSpec(memory_space=pltpu.SMEM)


def row_shift(step_z, step_y):
    return [
        (z * side + y, (z + step_z) % side * side + (y + step_y) % side)
        for z in range(side)
        for y in range(side)
    ]


def col_shift(step_x, step_core):
    return [
        (x * cores + k, (x + step_x) % side * cores + (k + step_core) % cores)
        for x in range(side)
        for k in range(cores)
    ]


def from_z(value, step):
    return lax.ppermute(value, "row", row_shift(-step, 0))


def from_y(value, step):
    return lax.ppermute(value, "row", row_shift(0, -step))


def back(step):
    return (side - step) % side


def half_at(number, half):
    return pl.ds(pl.multiple_of(number * half, half), half)


def spot_of(d, j, half):
    return slice((d * picks + j) * half, (d * picks + j + 1) * half)


def split(feature_ref, need_ref, *refs):
    outs, (need, sems) = refs[:-2], refs[-2:]
    half = lanes // 2
    rows = feature_ref.shape[0] // 2
    copies = [pltpu.make_async_copy(need_ref, need, sems.at[0])]
    for at, out in enumerate(outs):
        group, place = at // 2, at % 2
        for block in range(rows // half):
            start = (2 * block + place) * half
            copies.append(
                pltpu.make_async_copy(
                    feature_ref.at[start : start + half, group * span : (group + 1) * span],
                    out.at[block * half : (block + 1) * half, :],
                    sems.at[len(copies)],
                )
            )
    for copy in copies:
        copy.start()
    copies[0].wait()
    note = need[...].astype(jnp.float32)
    for out in outs[:2]:
        out[rows:, :] = jnp.zeros((note_rows, span), jnp.float32)
        out[rows : rows + note.shape[0], : note.shape[1]] = note
    for copy in copies[1:]:
        copy.wait()


def join(keep_ref, arrived_ref, mine_ref, right_ref, left_ref, over_right_ref, over_left_ref):
    size = mine_ref.shape[0]
    cut = size // 2
    for at, out in enumerate((mine_ref, right_ref, None, left_ref)):
        spot = slice(at * size, (at + 1) * size)
        if out is None:
            first, last = slice(at * size, at * size + cut), slice(at * size + cut, spot.stop)
            over_right_ref[...] = keep_ref[first] + arrived_ref[first]
            over_left_ref[...] = keep_ref[last] + arrived_ref[last]
        else:
            out[...] = keep_ref[spot] + arrived_ref[spot]


def relay(right_ref, left_ref, from_left_ref, from_right_ref, right_out, left_out):
    cut = from_left_ref.shape[0]
    right_out[:cut] = right_ref[:cut] + from_left_ref[...]
    left_out[cut:] = left_ref[cut:] + from_right_ref[...]


def log(value):
    return value.bit_length() - 1


def pairs_of(tile_total, blocks):
    return (tile_total + blocks) // 2 + unroll


def plan(row_ref, col_ref, count_ref, plan_ref, waiting, blocks_dev):
    tile_total = row_ref.shape[0]
    blocks = side * blocks_dev
    entries = pairs_of(tile_total, blocks)
    slot_bits = log(tile_total)
    code_bits = slot_bits + log(side * side * picks) + 1
    empty = (side * side * picks) << slot_bits
    my_z = lax.axis_index("row") // side
    my_y = lax.axis_index("row") % side
    my_x = lax.axis_index("col") // cores
    my_core = lax.axis_index("col") % cores

    def pair(place, first, second):
        return first | (second << code_bits) | (place << (2 * code_bits))

    for place in range(2 * blocks):
        waiting[place] = -1

    def turn(slot, ends):
        target = row_ref[slot]
        source = col_ref[slot]
        column = lax.shift_right_logical(target, log(blocks_dev))
        away_x = (lax.shift_right_logical(column, log(cores)) - my_x) & (side - 1)
        place = away_x * blocks_dev + (target & (blocks_dev - 1))
        kept = 1 - ((column & (cores - 1)) ^ my_core)
        owner = lax.shift_right_logical(source, log(picks))
        away_z = (lax.shift_right_logical(owner, log(side)) - my_z) & (side - 1)
        away_y = (owner - my_y) & (side - 1)
        pos = (away_z * side + away_y) * picks + (source & (picks - 1))
        code = slot | (pos << slot_bits)
        before = waiting[kept * blocks + place]
        full = (before >= 0).astype(jnp.int32)
        end = jnp.where(kept == 1, ends[1], ends[0])
        plan_ref[kept * entries + end] = pair(place, before, code)
        waiting[kept * blocks + place] = jnp.where(before >= 0, -1, code)
        return ends[0] + full * (1 - kept), ends[1] + full * kept

    ends = list(lax.fori_loop(0, count_ref[0, 0], turn, (0, 0)))
    for kept in range(2):
        for place in range(blocks):
            before = waiting[kept * blocks + place]
            plan_ref[kept * entries + ends[kept]] = pair(place, before, empty)
            ends[kept] = ends[kept] + (before >= 0).astype(jnp.int32)
        for extra in range(unroll):
            plan_ref[kept * entries + ends[kept] + extra] = pair(0, empty, empty)
        plan_ref[2 * entries + kept] = ends[kept]


def pack(half, *refs):
    first, second = refs[:side], refs[side : 2 * side]
    notes_from = refs[2 * side : 4 * side - 2]
    outs = refs[4 * side - 2 : 6 * side - 4]
    notes, sems = refs[6 * side - 4 :]
    rows = side * half
    copies = [
        pltpu.make_async_copy(
            source.at[rows : rows + note_rows, :lanes], notes.at[at], sems.at[at]
        )
        for at, source in enumerate(notes_from)
    ]
    for copy in copies:
        copy.start()
    for copy in copies:
        copy.wait()
    my_z = lax.axis_index("row") // side
    my_y = lax.axis_index("row") % side
    for away in range(1, side):
        for d in range(side):
            next_y = lax.rem(my_y + d, side)
            next_z = lax.rem(my_z + d, side)
            for j in range(picks):
                spot = spot_of(d, j, half)
                along_z = notes[away - 1, j, my_z * side + next_y].astype(jnp.int32)
                outs[away - 1][spot, :] = first[d][half_at(along_z, half), :]
                along_y = notes[side + away - 2, j, next_z * side + my_y].astype(jnp.int32)
                outs[side + away - 2][spot, :] = second[d][half_at(along_y, half), :]


def pack_group(first, second, notes, half):
    packed = jax.ShapeDtypeStruct((side * picks * half, span), jnp.float32)
    number = 2 * (side - 1)
    return pl.pallas_call(
        lambda *refs: pack(half, *refs),
        in_specs=[in_vmem] * (2 * side + number),
        out_specs=[in_vmem] * number,
        scratch_shapes=[
            pltpu.SMEM((number, note_rows, lanes), jnp.float32),
            pltpu.SemaphoreType.DMA((number,)),
        ],
        out_shape=[packed] * number,
        compiler_params=pltpu.CompilerParams(vmem_limit_bytes=5 << 20),
        cost_estimate=pl.CostEstimate(flops=0, bytes_accessed=5 << 20, transcendentals=0),
        name="pack",
    )(*first, *second, *notes)


def add_tiles(kept, plan_ref, tile_ref, pool, total):
    tile_total = tile_ref.shape[0]
    sources = pool.shape[0] - 1
    entries = pairs_of(tile_total, total.shape[0])
    slot_bits = log(tile_total)
    pos_bits = log(sources) + 1
    total[...] = jnp.zeros_like(total)

    def turn(step, carry):
        products = []
        for lane in range(unroll):
            code = plan_ref[kept * entries + step * unroll + lane]
            left, right = [], []
            for _ in range(2):
                left.append(tile_ref[code & (tile_total - 1)].astype(jnp.bfloat16))
                code = lax.shift_right_logical(code, slot_bits)
                right.append(pool[code & ((1 << pos_bits) - 1)])
                code = lax.shift_right_logical(code, pos_bits)
            product = jnp.dot(
                jnp.concatenate(left, axis=1),
                jnp.concatenate(right, axis=0),
                preferred_element_type=jnp.float32,
            )
            products.append((code, product))
        for target, product in products:
            total[target] += product
        return carry

    count = plan_ref[2 * entries + kept]
    lax.fori_loop(0, (count + unroll - 1) // unroll, turn, 0)


def combine(plan_ref, need_ref, tile_ref, *refs):
    first, second = refs[:side], refs[side : 2 * side]
    along_z = refs[2 * side : 3 * side - 1]
    along_y = refs[3 * side - 1 : 4 * side - 2]
    total, pool = refs[4 * side - 2 :]
    half = pool.shape[1] // 2
    top, low = slice(0, half), slice(half, 2 * half)
    my_z = lax.axis_index("row") // side
    my_y = lax.axis_index("row") % side
    for d in range(side):
        next_y = lax.rem(my_y + d, side)
        next_z = lax.rem(my_z + d, side)
        for j in range(picks):
            mine = need_ref[j, my_z * side + next_y]
            pool[d * picks + j, top, :] = first[d][half_at(mine, half), :].astype(pool.dtype)
            mine = need_ref[j, next_z * side + my_y]
            pool[d * side * picks + j, low, :] = second[d][half_at(mine, half), :].astype(
                pool.dtype
            )
            spot = spot_of(d, j, half)
            for away in range(1, side):
                pool[(back(away) * side + d) * picks + j, top, :] = along_z[away - 1][
                    spot, :
                ].astype(pool.dtype)
                pool[(d * side + back(away)) * picks + j, low, :] = along_y[away - 1][
                    spot, :
                ].astype(pool.dtype)
    pool[side * side * picks] = jnp.zeros(pool.shape[1:], pool.dtype)
    add_tiles(0, plan_ref, tile_ref, pool, total)


def combine_sent(listed, need, tiles, first, second, along_z, along_y, blocks):
    edge = tiles.shape[1]
    return pl.pallas_call(
        combine,
        in_specs=[in_smem] * 2 + [in_vmem] * (4 * side - 1),
        out_specs=[in_vmem] * 2,
        out_shape=[
            jax.ShapeDtypeStruct((blocks, edge, span), jnp.float32),
            jax.ShapeDtypeStruct((side * side * picks + 1, edge, span), jnp.bfloat16),
        ],
        compiler_params=pltpu.CompilerParams(vmem_limit_bytes=10 << 20),
        cost_estimate=pl.CostEstimate(flops=2 << 30, bytes_accessed=10 << 20, transcendentals=0),
        name="combine",
    )(listed, need, tiles, *first, *second, *along_z, *along_y)


def combine_kept(listed, tiles, pool, blocks):
    edge = tiles.shape[1]
    return pl.pallas_call(
        lambda plan_ref, tile_ref, pool, total: add_tiles(1, plan_ref, tile_ref, pool, total),
        in_specs=[in_smem] + [in_vmem] * 2,
        out_specs=in_vmem,
        out_shape=jax.ShapeDtypeStruct((blocks, edge, span), jnp.float32),
        compiler_params=pltpu.CompilerParams(vmem_limit_bytes=6 << 20),
        cost_estimate=pl.CostEstimate(flops=2 << 30, bytes_accessed=8 << 20, transcendentals=0),
        name="keep",
    )(listed, tiles, pool)


def mixed_of(group, feature_ref, totals):
    part = slice(group * span, (group + 1) * span)
    summed = totals[0][...]
    for other in totals[1:]:
        summed = summed + other[...]
    return ((1.0 + gin_epsilon) * feature_ref[:, part] + summed).astype(jnp.bfloat16)


def begin_mlp(feature_ref, w_ref, bias_ref, *refs):
    totals, out_ref, mixed = refs[:parts], refs[parts], refs[parts + 1]
    mixed[...] = mixed_of(0, feature_ref, totals)

    def turn(step, carry):
        part = pl.ds(pl.multiple_of(step * chunk, chunk), chunk)
        out_ref[:, part] = (
            jnp.dot(mixed[...], w_ref[:span, part], preferred_element_type=jnp.float32)
            + bias_ref[:, part]
        )
        return carry

    lax.fori_loop(0, w_ref.shape[1] // chunk, turn, 0)


def end_mlp(feature_ref, w_ref, before_ref, w_out_ref, bias_ref, *refs):
    totals, out_ref, mixed, total = refs[:parts], refs[parts], refs[parts + 1], refs[parts + 2]
    mixed[...] = mixed_of(1, feature_ref, totals)
    total[...] = jnp.broadcast_to(bias_ref[...], total.shape)

    def turn(step, carry):
        part = pl.ds(pl.multiple_of(step * chunk, chunk), chunk)
        hidden = before_ref[:, part] + jnp.dot(
            mixed[...], w_ref[span:, part], preferred_element_type=jnp.float32
        )
        hidden = jnp.maximum(hidden, 0.0).astype(jnp.bfloat16)
        total[...] += jnp.dot(hidden, w_out_ref[part, :], preferred_element_type=jnp.float32)
        return carry

    lax.fori_loop(0, w_ref.shape[1] // chunk, turn, 0)
    out_ref[...] = total[...].astype(out_ref.dtype)


def on_device(
    features, tiles, tile_rows, tile_cols, tile_count, needed, w_in, bias_in, w_out, bias_out
):
    edge = tiles.shape[-1]
    half = edge // 2
    nodes, width = features.shape
    blocks_dev = nodes // edge
    hidden_size = w_in.shape[1]
    blocks = side * blocks_dev
    groups = width // span
    rows = nodes // 2

    need = needed[0, 0].T
    payload = [
        jax.ShapeDtypeStruct((rows + (note_rows if group == 0 else 0), span), jnp.float32)
        for group in range(groups)
        for _ in range(2)
    ]
    own = pl.pallas_call(
        split,
        in_specs=[pl.BlockSpec(memory_space=pltpu.HBM)] * 2,
        out_specs=[in_vmem] * len(payload),
        scratch_shapes=[
            pltpu.VMEM(need.shape, jnp.int32),
            pltpu.SemaphoreType.DMA((1 + len(payload) * blocks_dev,)),
        ],
        out_shape=payload,
        compiler_params=pltpu.CompilerParams(vmem_limit_bytes=4 << 20),
        cost_estimate=pl.CostEstimate(flops=0, bytes_accessed=2 << 20, transcendentals=0),
        name="split",
    )(features, need)
    firsts, seconds = [], []
    for group in range(groups):
        first = [own[2 * group]] + [None] * (side - 1)
        second = [own[2 * group + 1]] + [None] * (side - 1)
        for away in (1, 3, 2):
            first[away] = from_y(first[0], away)
            second[away] = from_z(second[0], away)
        firsts.append(first)
        seconds.append(second)
    notes = seconds[0][1:] + firsts[0][1:]

    listed = pl.pallas_call(
        lambda *refs: plan(*refs, blocks_dev),
        in_specs=[in_smem] * 3,
        out_specs=in_smem,
        out_shape=jax.ShapeDtypeStruct((256,), jnp.int32),
        scratch_shapes=[pltpu.SMEM((2 * blocks,), jnp.int32)],
        compiler_params=pltpu.CompilerParams(vmem_limit_bytes=1 << 20),
        cost_estimate=pl.CostEstimate(flops=0, bytes_accessed=1 << 20, transcendentals=0),
        name="plan",
    )(tile_rows[0, 0], tile_cols[0, 0], tile_count)
    cell_tiles = tiles[0, 0]

    sums = []
    for group in range(groups):
        first, second = firsts[group], seconds[group]
        packed = pack_group(first, second, notes, half)
        along_z, along_y = [None] * (side - 1), [None] * (side - 1)
        for away in (1, 3, 2):
            along_z[away - 1] = from_z(packed[away - 1], -away)
            along_y[away - 1] = from_y(packed[side + away - 2], -away)
        send, pool = combine_sent(listed, need, cell_tiles, first, second, along_z, along_y, blocks)
        arrived = lax.ppermute(send, "col", col_shift(0, 1))
        keep = combine_kept(listed, cell_tiles, pool, blocks)
        full = jax.ShapeDtypeStruct((blocks_dev, edge, span), jnp.float32)
        part = jax.ShapeDtypeStruct((blocks_dev // 2, edge, span), jnp.float32)
        mine, right, left, over_right, over_left = pl.pallas_call(
            join,
            in_specs=[in_vmem] * 2,
            out_specs=[in_vmem] * 5,
            out_shape=[full] * 3 + [part] * 2,
            compiler_params=pltpu.CompilerParams(vmem_limit_bytes=6 << 20),
            cost_estimate=pl.CostEstimate(flops=0, bytes_accessed=4 << 20, transcendentals=0),
            name="join",
        )(keep, arrived)
        relay_right = lax.ppermute(over_right, "col", col_shift(1, 0))
        relay_left = lax.ppermute(over_left, "col", col_shift(-1, 0))
        right, left = pl.pallas_call(
            relay,
            in_specs=[in_vmem] * 4,
            out_specs=[in_vmem] * 2,
            out_shape=[full] * 2,
            input_output_aliases={0: 0, 1: 1},
            compiler_params=pltpu.CompilerParams(vmem_limit_bytes=5 << 20),
            cost_estimate=pl.CostEstimate(flops=0, bytes_accessed=2 << 20, transcendentals=0),
            name="relay",
        )(right, left, relay_right, relay_left)
        from_left = lax.ppermute(right, "col", col_shift(1, 0))
        from_right = lax.ppermute(left, "col", col_shift(-1, 0))
        sums.append([v.reshape(nodes, span) for v in (mine, from_left, from_right)])

    before = pl.pallas_call(
        begin_mlp,
        in_specs=[in_vmem] * (3 + parts),
        out_specs=in_vmem,
        out_shape=jax.ShapeDtypeStruct((nodes, hidden_size), jnp.float32),
        scratch_shapes=[pltpu.VMEM((nodes, span), jnp.bfloat16)],
        compiler_params=pltpu.CompilerParams(vmem_limit_bytes=8 << 20),
        cost_estimate=pl.CostEstimate(
            flops=1 << 29, bytes_accessed=8 << 20, transcendentals=0
        ),
        name="begin",
    )(features, w_in, bias_in.reshape(1, -1), *sums[0])
    return pl.pallas_call(
        end_mlp,
        in_specs=[in_vmem] * (5 + parts),
        out_specs=in_vmem,
        out_shape=jax.ShapeDtypeStruct((nodes, width), jnp.bfloat16),
        scratch_shapes=[
            pltpu.VMEM((nodes, span), jnp.bfloat16),
            pltpu.VMEM((nodes, width), jnp.float32),
        ],
        compiler_params=pltpu.CompilerParams(vmem_limit_bytes=6 << 20),
        cost_estimate=pl.CostEstimate(
            flops=3 << 29, bytes_accessed=8 << 20, transcendentals=0
        ),
        name="end",
    )(features, w_in, before, w_out, bias_out.reshape(1, -1), *sums[1])


def solution(mesh):
    placed = (
        P(("row", "col"), None),
        P("row", "col", None, None, None),
        P("row", "col", None),
        P("row", "col", None),
        P("row", "col"),
        P("row", "col", None, None),
        P(),
        P(),
        P(),
        P(),
    )

    return jax.shard_map(
        on_device, mesh=mesh, in_specs=placed, out_specs=P(("row", "col"), None), check_vma=False
    )
```

```python
import jax
import jax.numpy as jnp
from jax import lax
from jax.experimental import pallas as pl
from jax.experimental.pallas import tpu as pltpu
from jax.sharding import PartitionSpec as P


gin_epsilon = 0.25
unroll = 8
span = 256
side = 4
cores = 2
picks = 2
lists = 4
across_x = side // 2
note_rows = 8
lanes = 128
chunk = 256

in_vmem = pl.BlockSpec(memory_space=pltpu.VMEM)
in_smem = pl.BlockSpec(memory_space=pltpu.SMEM)


def row_shift(step_z, step_y):
    return [
        (z * side + y, (z + step_z) % side * side + (y + step_y) % side)
        for z in range(side)
        for y in range(side)
    ]


def col_shift(step_x, step_core):
    return [
        (x * cores + k, (x + step_x) % side * cores + (k + step_core) % cores)
        for x in range(side)
        for k in range(cores)
    ]


def from_z(value, step):
    return lax.ppermute(value, "row", row_shift(-step, 0))


def from_y(value, step):
    return lax.ppermute(value, "row", row_shift(0, -step))


def back(step):
    return (side - step) % side


def half_at(number, half):
    return pl.ds(pl.multiple_of(number * half, half), half)


def spot_of(d, j, half):
    return slice((d * picks + j) * half, (d * picks + j + 1) * half)


def split(feature_ref, need_ref, *refs):
    outs, (need, sems) = refs[:-2], refs[-2:]
    half = lanes // 2
    rows = feature_ref.shape[0] // 2
    copies = [pltpu.make_async_copy(need_ref, need, sems.at[0])]
    for at, out in enumerate(outs):
        group, place = at // 2, at % 2
        for block in range(rows // half):
            start = (2 * block + place) * half
            copies.append(
                pltpu.make_async_copy(
                    feature_ref.at[start : start + half, group * span : (group + 1) * span],
                    out.at[block * half : (block + 1) * half, :],
                    sems.at[len(copies)],
                )
            )
    for copy in copies:
        copy.start()
    copies[0].wait()
    note = need[...].astype(jnp.float32)
    for out in outs[:2]:
        out[rows:, :] = jnp.zeros((note_rows, span), jnp.float32)
        out[rows : rows + note.shape[0], : note.shape[1]] = note
    for copy in copies[1:]:
        copy.wait()


def join_across(keep_ref, arrived_ref, over_right_ref, over_left_ref):
    cut = over_right_ref.shape[0]
    over_right_ref[...] = keep_ref[:cut] + arrived_ref[:cut]
    over_left_ref[...] = keep_ref[cut:] + arrived_ref[cut:]


def join_rest(keep_ref, arrived_ref, *outs):
    start = 0
    for out in outs:
        spot = slice(start, start + out.shape[0])
        out[...] = keep_ref[spot] + arrived_ref[spot]
        start = spot.stop


def relay(right_ref, left_ref, from_left_ref, from_right_ref, right_out, left_out):
    right_out[...] = right_ref[...] + from_left_ref[...]
    left_out[...] = left_ref[...] + from_right_ref[...]


def log(value):
    return value.bit_length() - 1


def places_of(which, blocks_dev):
    return blocks_dev * (1 if which % 2 == 0 else side - 1)


def pairs_of(tile_total, blocks_dev):
    return (tile_total + places_of(1, blocks_dev)) // 2 + unroll


def plan(row_ref, col_ref, count_ref, plan_ref, waiting, blocks_dev):
    tile_total = row_ref.shape[0]
    blocks = places_of(1, blocks_dev)
    entries = pairs_of(tile_total, blocks_dev)
    slot_bits = log(tile_total)
    code_bits = slot_bits + log(side * side * picks) + 1
    empty = (side * side * picks) << slot_bits
    my_z = lax.axis_index("row") // side
    my_y = lax.axis_index("row") % side
    my_x = lax.axis_index("col") // cores
    my_core = lax.axis_index("col") % cores

    def pair(place, first, second):
        return first | (second << code_bits) | (place << (2 * code_bits))

    for place in range(lists * blocks):
        waiting[place] = -1
    for which in range(lists):
        waiting[lists * blocks + which] = 0

    def turn(slot, carry):
        target = row_ref[slot]
        source = col_ref[slot]
        column = lax.shift_right_logical(target, log(blocks_dev))
        away_x = (lax.shift_right_logical(column, log(cores)) - my_x) & (side - 1)
        across = (away_x == across_x).astype(jnp.int32)
        order_x = jnp.where(across == 1, 0, away_x - (away_x > across_x).astype(jnp.int32))
        place = order_x * blocks_dev + (target & (blocks_dev - 1))
        which = 2 * (1 - ((column & (cores - 1)) ^ my_core)) + 1 - across
        owner = lax.shift_right_logical(source, log(picks))
        away_z = (lax.shift_right_logical(owner, log(side)) - my_z) & (side - 1)
        away_y = (owner - my_y) & (side - 1)
        pos = (away_z * side + away_y) * picks + (source & (picks - 1))
        code = slot | (pos << slot_bits)
        before = waiting[which * blocks + place]
        end = waiting[lists * blocks + which]
        plan_ref[which * entries + end] = pair(place, before, code)
        waiting[which * blocks + place] = jnp.where(before >= 0, -1, code)
        waiting[lists * blocks + which] = end + (before >= 0).astype(jnp.int32)
        return carry

    lax.fori_loop(0, count_ref[0, 0], turn, 0)
    for which in range(lists):
        end = waiting[lists * blocks + which]
        for place in range(places_of(which, blocks_dev)):
            before = waiting[which * blocks + place]
            plan_ref[which * entries + end] = pair(place, before, empty)
            end = end + (before >= 0).astype(jnp.int32)
        for extra in range(unroll):
            plan_ref[which * entries + end + extra] = pair(0, empty, empty)
        plan_ref[lists * entries + which] = end


def pack(half, *refs):
    first, second = refs[:side], refs[side : 2 * side]
    notes_from = refs[2 * side : 4 * side - 2]
    outs = refs[4 * side - 2 : 6 * side - 4]
    notes, sems = refs[6 * side - 4 :]
    rows = side * half
    copies = [
        pltpu.make_async_copy(
            source.at[rows : rows + note_rows, :lanes], notes.at[at], sems.at[at]
        )
        for at, source in enumerate(notes_from)
    ]
    for copy in copies:
        copy.start()
    for copy in copies:
        copy.wait()
    my_z = lax.axis_index("row") // side
    my_y = lax.axis_index("row") % side
    for away in range(1, side):
        for d in range(side):
            next_y = lax.rem(my_y + d, side)
            next_z = lax.rem(my_z + d, side)
            for j in range(picks):
                spot = spot_of(d, j, half)
                along_z = notes[away - 1, j, my_z * side + next_y].astype(jnp.int32)
                outs[away - 1][spot, :] = first[d][half_at(along_z, half), :]
                along_y = notes[side + away - 2, j, next_z * side + my_y].astype(jnp.int32)
                outs[side + away - 2][spot, :] = second[d][half_at(along_y, half), :]


def pack_group(first, second, notes, half):
    packed = jax.ShapeDtypeStruct((side * picks * half, span), jnp.float32)
    number = 2 * (side - 1)
    return pl.pallas_call(
        lambda *refs: pack(half, *refs),
        in_specs=[in_vmem] * (2 * side + number),
        out_specs=[in_vmem] * number,
        scratch_shapes=[
            pltpu.SMEM((number, note_rows, lanes), jnp.float32),
            pltpu.SemaphoreType.DMA((number,)),
        ],
        out_shape=[packed] * number,
        compiler_params=pltpu.CompilerParams(vmem_limit_bytes=5 << 20),
        cost_estimate=pl.CostEstimate(flops=0, bytes_accessed=5 << 20, transcendentals=0),
        name="pack",
    )(*first, *second, *notes)


def add_tiles(which, blocks_dev, plan_ref, tile_ref, pool, total):
    tile_total = tile_ref.shape[0]
    sources = pool.shape[0] - 1
    entries = pairs_of(tile_total, blocks_dev)
    slot_bits = log(tile_total)
    pos_bits = log(sources) + 1
    total[...] = jnp.zeros_like(total)

    def turn(step, carry):
        products = []
        for lane in range(unroll):
            code = plan_ref[which * entries + step * unroll + lane]
            left, right = [], []
            for _ in range(2):
                left.append(tile_ref[code & (tile_total - 1)].astype(jnp.bfloat16))
                code = lax.shift_right_logical(code, slot_bits)
                right.append(pool[code & ((1 << pos_bits) - 1)])
                code = lax.shift_right_logical(code, pos_bits)
            product = jnp.dot(
                jnp.concatenate(left, axis=1),
                jnp.concatenate(right, axis=0),
                preferred_element_type=jnp.float32,
            )
            products.append((code, product))
        for target, product in products:
            total[target] += product
        return carry

    count = plan_ref[lists * entries + which]
    lax.fori_loop(0, (count + unroll - 1) // unroll, turn, 0)


def combine(blocks_dev, plan_ref, need_ref, tile_ref, *refs):
    first, second = refs[:side], refs[side : 2 * side]
    along_z = refs[2 * side : 3 * side - 1]
    along_y = refs[3 * side - 1 : 4 * side - 2]
    total, pool = refs[4 * side - 2 :]
    half = pool.shape[1] // 2
    top, low = slice(0, half), slice(half, 2 * half)
    my_z = lax.axis_index("row") // side
    my_y = lax.axis_index("row") % side
    for d in range(side):
        next_y = lax.rem(my_y + d, side)
        next_z = lax.rem(my_z + d, side)
        for j in range(picks):
            mine = need_ref[j, my_z * side + next_y]
            pool[d * picks + j, top, :] = first[d][half_at(mine, half), :].astype(pool.dtype)
            mine = need_ref[j, next_z * side + my_y]
            pool[d * side * picks + j, low, :] = second[d][half_at(mine, half), :].astype(
                pool.dtype
            )
            spot = spot_of(d, j, half)
            for away in range(1, side):
                pool[(back(away) * side + d) * picks + j, top, :] = along_z[away - 1][
                    spot, :
                ].astype(pool.dtype)
                pool[(d * side + back(away)) * picks + j, low, :] = along_y[away - 1][
                    spot, :
                ].astype(pool.dtype)
    pool[side * side * picks] = jnp.zeros(pool.shape[1:], pool.dtype)
    add_tiles(0, blocks_dev, plan_ref, tile_ref, pool, total)


def combine_sent(listed, need, tiles, first, second, along_z, along_y, blocks_dev):
    edge = tiles.shape[1]
    return pl.pallas_call(
        lambda *refs: combine(blocks_dev, *refs),
        in_specs=[in_smem] * 2 + [in_vmem] * (4 * side - 1),
        out_specs=[in_vmem] * 2,
        out_shape=[
            jax.ShapeDtypeStruct((places_of(0, blocks_dev), edge, span), jnp.float32),
            jax.ShapeDtypeStruct((side * side * picks + 1, edge, span), jnp.bfloat16),
        ],
        compiler_params=pltpu.CompilerParams(vmem_limit_bytes=10 << 20),
        cost_estimate=pl.CostEstimate(flops=2 << 30, bytes_accessed=10 << 20, transcendentals=0),
        name="combine",
    )(listed, need, tiles, *first, *second, *along_z, *along_y)


def combine_listed(which, listed, tiles, pool, blocks_dev):
    edge = tiles.shape[1]
    return pl.pallas_call(
        lambda *refs: add_tiles(which, blocks_dev, *refs),
        in_specs=[in_smem] + [in_vmem] * 2,
        out_specs=in_vmem,
        out_shape=jax.ShapeDtypeStruct((places_of(which, blocks_dev), edge, span), jnp.float32),
        compiler_params=pltpu.CompilerParams(vmem_limit_bytes=6 << 20),
        cost_estimate=pl.CostEstimate(flops=2 << 30, bytes_accessed=8 << 20, transcendentals=0),
        name="listed",
    )(listed, tiles, pool)


def mix(group, feature_ref, totals, mixed):
    part = slice(group * span, (group + 1) * span)
    mine, rest = totals[0], totals[1:]
    rows = rest[0].shape[0]
    for at in range(2):
        spot = slice(at * rows, (at + 1) * rows)
        summed = mine[spot, :] + rest[2 * at][...] + rest[2 * at + 1][...]
        mixed[spot, :] = ((1.0 + gin_epsilon) * feature_ref[spot, part] + summed).astype(mixed.dtype)


def begin_mlp(feature_ref, w_ref, bias_ref, *refs):
    totals, (out_ref, mixed) = refs[:-2], refs[-2:]
    mix(0, feature_ref, totals, mixed)

    def turn(step, carry):
        part = pl.ds(pl.multiple_of(step * chunk, chunk), chunk)
        out_ref[part, :] = (
            jnp.dot(mixed[part, :], w_ref[:span, :], preferred_element_type=jnp.float32)
            + bias_ref[...]
        )
        return carry

    lax.fori_loop(0, out_ref.shape[0] // chunk, turn, 0)


def end_mlp(feature_ref, w_ref, before_ref, w_out_ref, bias_ref, *refs):
    totals, (out_ref, mixed) = refs[:-2], refs[-2:]
    mix(1, feature_ref, totals, mixed)

    def turn(step, carry):
        part = pl.ds(pl.multiple_of(step * chunk, chunk), chunk)
        hidden = before_ref[part, :] + jnp.dot(
            mixed[part, :], w_ref[span:, :], preferred_element_type=jnp.float32
        )
        hidden = jnp.maximum(hidden, 0.0).astype(jnp.bfloat16)
        updated = jnp.dot(hidden, w_out_ref[...], preferred_element_type=jnp.float32)
        out_ref[part, :] = (updated + bias_ref[...]).astype(out_ref.dtype)
        return carry

    lax.fori_loop(0, out_ref.shape[0] // chunk, turn, 0)


def on_device(
    features, tiles, tile_rows, tile_cols, tile_count, needed, w_in, bias_in, w_out, bias_out
):
    edge = tiles.shape[-1]
    half = edge // 2
    nodes, width = features.shape
    blocks_dev = nodes // edge
    hidden_size = w_in.shape[1]
    blocks = places_of(1, blocks_dev)
    groups = width // span
    rows = nodes // 2

    need = needed[0, 0].T
    payload = [
        jax.ShapeDtypeStruct((rows + (note_rows if group == 0 else 0), span), jnp.float32)
        for group in range(groups)
        for _ in range(2)
    ]
    own = pl.pallas_call(
        split,
        in_specs=[pl.BlockSpec(memory_space=pltpu.HBM)] * 2,
        out_specs=[in_vmem] * len(payload),
        scratch_shapes=[
            pltpu.VMEM(need.shape, jnp.int32),
            pltpu.SemaphoreType.DMA((1 + len(payload) * blocks_dev,)),
        ],
        out_shape=payload,
        compiler_params=pltpu.CompilerParams(vmem_limit_bytes=4 << 20),
        cost_estimate=pl.CostEstimate(flops=0, bytes_accessed=2 << 20, transcendentals=0),
        name="split",
    )(features, need)
    firsts, seconds = [], []
    for group in range(groups):
        first = [own[2 * group]] + [None] * (side - 1)
        second = [own[2 * group + 1]] + [None] * (side - 1)
        for away in (1, 3, 2):
            first[away] = from_y(first[0], away)
            second[away] = from_z(second[0], away)
        firsts.append(first)
        seconds.append(second)
    notes = seconds[0][1:] + firsts[0][1:]

    listed = pl.pallas_call(
        lambda *refs: plan(*refs, blocks_dev),
        in_specs=[in_smem] * 3,
        out_specs=in_smem,
        out_shape=jax.ShapeDtypeStruct((512,), jnp.int32),
        scratch_shapes=[pltpu.SMEM((lists * (blocks + 1),), jnp.int32)],
        compiler_params=pltpu.CompilerParams(vmem_limit_bytes=1 << 20),
        cost_estimate=pl.CostEstimate(flops=0, bytes_accessed=1 << 20, transcendentals=0),
        name="plan",
    )(tile_rows[0, 0], tile_cols[0, 0], tile_count)
    cell_tiles = tiles[0, 0]

    sums = []
    for group in range(groups):
        first, second = firsts[group], seconds[group]
        packed = pack_group(first, second, notes, half)
        along_z, along_y = [None] * (side - 1), [None] * (side - 1)
        for away in (1, 3, 2):
            along_z[away - 1] = from_z(packed[away - 1], -away)
            along_y[away - 1] = from_y(packed[side + away - 2], -away)
        send, pool = combine_sent(
            listed, need, cell_tiles, first, second, along_z, along_y, blocks_dev
        )
        arrived = lax.ppermute(send, "col", col_shift(0, 1))
        keep = combine_listed(2, listed, cell_tiles, pool, blocks_dev)
        over_right, over_left = pl.pallas_call(
            join_across,
            in_specs=[in_vmem] * 2,
            out_specs=[in_vmem] * 2,
            out_shape=[jax.ShapeDtypeStruct((blocks_dev // 2, edge, span), jnp.float32)] * 2,
            compiler_params=pltpu.CompilerParams(vmem_limit_bytes=4 << 20),
            cost_estimate=pl.CostEstimate(flops=0, bytes_accessed=2 << 20, transcendentals=0),
            name="join",
        )(keep, arrived)
        relay_right = lax.ppermute(over_right, "col", col_shift(1, 0))
        relay_left = lax.ppermute(over_left, "col", col_shift(-1, 0))
        send = combine_listed(1, listed, cell_tiles, pool, blocks_dev)
        arrived = lax.ppermute(send, "col", col_shift(0, 1))
        keep = combine_listed(3, listed, cell_tiles, pool, blocks_dev)
        cut = blocks_dev // 2
        sizes = (blocks_dev, cut, cut, cut, cut)
        mine, right_held, right, left, left_held = pl.pallas_call(
            join_rest,
            in_specs=[in_vmem] * 2,
            out_specs=[in_vmem] * len(sizes),
            out_shape=[jax.ShapeDtypeStruct((n, edge, span), jnp.float32) for n in sizes],
            compiler_params=pltpu.CompilerParams(vmem_limit_bytes=6 << 20),
            cost_estimate=pl.CostEstimate(flops=0, bytes_accessed=4 << 20, transcendentals=0),
            name="join",
        )(keep, arrived)
        from_left = lax.ppermute(right, "col", col_shift(1, 0))
        from_right = lax.ppermute(left, "col", col_shift(-1, 0))
        right_held, left_held = pl.pallas_call(
            relay,
            in_specs=[in_vmem] * 4,
            out_specs=[in_vmem] * 2,
            out_shape=[jax.ShapeDtypeStruct((cut, edge, span), jnp.float32)] * 2,
            compiler_params=pltpu.CompilerParams(vmem_limit_bytes=4 << 20),
            cost_estimate=pl.CostEstimate(flops=0, bytes_accessed=2 << 20, transcendentals=0),
            name="relay",
        )(right_held, left_held, relay_right, relay_left)
        from_left_held = lax.ppermute(right_held, "col", col_shift(1, 0))
        from_right_held = lax.ppermute(left_held, "col", col_shift(-1, 0))
        sums.append(
            [
                v.reshape(-1, span)
                for v in (mine, from_left_held, from_right, from_left, from_right_held)
            ]
        )

    before = pl.pallas_call(
        begin_mlp,
        in_specs=[in_vmem] * (3 + len(sums[0])),
        out_specs=in_vmem,
        out_shape=jax.ShapeDtypeStruct((nodes, hidden_size), jnp.float32),
        scratch_shapes=[pltpu.VMEM((nodes, span), jnp.bfloat16)],
        compiler_params=pltpu.CompilerParams(vmem_limit_bytes=8 << 20),
        cost_estimate=pl.CostEstimate(
            flops=1 << 29, bytes_accessed=8 << 20, transcendentals=0
        ),
        name="begin",
    )(features, w_in, bias_in.reshape(1, -1), *sums[0])
    return pl.pallas_call(
        end_mlp,
        in_specs=[in_vmem] * (5 + len(sums[1])),
        out_specs=in_vmem,
        out_shape=jax.ShapeDtypeStruct((nodes, width), jnp.bfloat16),
        scratch_shapes=[pltpu.VMEM((nodes, span), jnp.bfloat16)],
        compiler_params=pltpu.CompilerParams(vmem_limit_bytes=8 << 20),
        cost_estimate=pl.CostEstimate(
            flops=3 << 29, bytes_accessed=8 << 20, transcendentals=0
        ),
        name="end",
    )(features, w_in, before, w_out, bias_out.reshape(1, -1), *sums[1])


def solution(mesh):
    placed = (
        P(("row", "col"), None),
        P("row", "col", None, None, None),
        P("row", "col", None),
        P("row", "col", None),
        P("row", "col"),
        P("row", "col", None, None),
        P(),
        P(),
        P(),
        P(),
    )

    return jax.shard_map(
        on_device, mesh=mesh, in_specs=placed, out_specs=P(("row", "col"), None), check_vma=False
    )
```

```python
import jax
import jax.numpy as jnp
from jax import lax
from jax.experimental import pallas as pl
from jax.experimental.pallas import tpu as pltpu
from jax.sharding import PartitionSpec as P


gin_epsilon = 0.25
unroll = 8
span = 256
side = 4
cores = 2
picks = 2
kinds = 3
across_x = side // 2
note_rows = 8
lanes = 128
chunk = 256

in_vmem = pl.BlockSpec(memory_space=pltpu.VMEM)
in_smem = pl.BlockSpec(memory_space=pltpu.SMEM)


def row_shift(step_z, step_y):
    return [
        (z * side + y, (z + step_z) % side * side + (y + step_y) % side)
        for z in range(side)
        for y in range(side)
    ]


def col_shift(step_x, step_core):
    return [
        (x * cores + k, (x + step_x) % side * cores + (k + step_core) % cores)
        for x in range(side)
        for k in range(cores)
    ]


def from_z(value, step):
    return lax.ppermute(value, "row", row_shift(-step, 0))


def from_y(value, step):
    return lax.ppermute(value, "row", row_shift(0, -step))


def back(step):
    return (side - step) % side


def half_at(number, half):
    return pl.ds(pl.multiple_of(number * half, half), half)


def spot_of(d, j, half):
    return slice((d * picks + j) * half, (d * picks + j + 1) * half)


def split(group, feature_ref, *refs):
    noted = group == 0
    if noted:
        need_ref, first_ref, second_ref, need, sems = refs
    else:
        first_ref, second_ref, sems = refs
    half = lanes // 2
    rows = feature_ref.shape[0] // 2
    part = slice(group * span, (group + 1) * span)
    copies = []
    for place, out in enumerate((first_ref, second_ref)):
        for block in range(rows // half):
            start = (2 * block + place) * half
            copies.append(
                pltpu.make_async_copy(
                    feature_ref.at[start : start + half, part],
                    out.at[block * half : (block + 1) * half, :],
                    sems.at[len(copies)],
                )
            )
    if noted:
        copy = pltpu.make_async_copy(need_ref, need, sems.at[len(copies)])
        copy.start()
    for each in copies:
        each.start()
    if noted:
        copy.wait()
        note = need[...].astype(jnp.float32)
        for out in (first_ref, second_ref):
            out[rows:, :] = jnp.zeros((note_rows, span), jnp.float32)
            out[rows : rows + note.shape[0], : note.shape[1]] = note
    for each in copies:
        each.wait()


def split_group(group, features, need):
    nodes = features.shape[0]
    args = [features] + ([need] if group == 0 else [])
    rows = nodes // 2 + (note_rows if group == 0 else 0)
    copies = nodes // lanes * 2 + (1 if group == 0 else 0)
    return pl.pallas_call(
        lambda *refs: split(group, *refs),
        in_specs=[pl.BlockSpec(memory_space=pltpu.HBM)] * len(args),
        out_specs=[in_vmem] * 2,
        scratch_shapes=([pltpu.VMEM(need.shape, jnp.int32)] if group == 0 else [])
        + [pltpu.SemaphoreType.DMA((copies,))],
        out_shape=[jax.ShapeDtypeStruct((rows, span), jnp.float32)] * 2,
        compiler_params=pltpu.CompilerParams(vmem_limit_bytes=4 << 20),
        cost_estimate=pl.CostEstimate(flops=0, bytes_accessed=1 << 20, transcendentals=0),
        name="split",
    )(*[pltpu.with_memory_space_constraint(v, pltpu.HBM) for v in args])


def join_across(keep_ref, arrived_ref, over_right_ref, over_left_ref):
    cut = over_right_ref.shape[0]
    over_right_ref[...] = keep_ref[:cut] + arrived_ref[:cut]
    over_left_ref[...] = keep_ref[cut:] + arrived_ref[cut:]


def join_rest(keep_ref, arrived_ref, *outs):
    start = 0
    for out in outs:
        spot = slice(start, start + out.shape[0])
        out[...] = keep_ref[spot] + arrived_ref[spot]
        start = spot.stop


def relay(right_ref, left_ref, from_left_ref, from_right_ref, right_out, left_out):
    right_out[...] = right_ref[...] + from_left_ref[...]
    left_out[...] = left_ref[...] + from_right_ref[...]


def log(value):
    return value.bit_length() - 1


def places_of(which, blocks_dev):
    return blocks_dev * (2 if which % kinds == 1 else 1)


def pairs_of(tile_total, blocks_dev):
    return (tile_total + places_of(1, blocks_dev)) // 2 + unroll


def plan(row_ref, col_ref, count_ref, plan_ref, waiting, blocks_dev):
    tile_total = row_ref.shape[0]
    blocks = places_of(1, blocks_dev)
    entries = pairs_of(tile_total, blocks_dev)
    slot_bits = log(tile_total)
    code_bits = slot_bits + log(side * side * picks) + 1
    empty = (side * side * picks) << slot_bits
    my_z = lax.axis_index("row") // side
    my_y = lax.axis_index("row") % side
    my_x = lax.axis_index("col") // cores
    my_core = lax.axis_index("col") % cores

    def pair(place, first, second):
        return first | (second << code_bits) | (place << (2 * code_bits))

    for place in range(2 * kinds * blocks):
        waiting[place] = -1
    for which in range(2 * kinds):
        waiting[2 * kinds * blocks + which] = 0

    def turn(slot, carry):
        target = row_ref[slot]
        source = col_ref[slot]
        column = lax.shift_right_logical(target, log(blocks_dev))
        away_x = (lax.shift_right_logical(column, log(cores)) - my_x) & (side - 1)
        beside = away_x & 1
        kind = jnp.where(beside == 1, 1, jnp.where(away_x == across_x, 0, 2))
        right = (away_x > across_x).astype(jnp.int32)
        place = right * blocks_dev + (target & (blocks_dev - 1))
        which = kinds * (1 - ((column & (cores - 1)) ^ my_core)) + kind
        owner = lax.shift_right_logical(source, log(picks))
        away_z = (lax.shift_right_logical(owner, log(side)) - my_z) & (side - 1)
        away_y = (owner - my_y) & (side - 1)
        pos = (away_z * side + away_y) * picks + (source & (picks - 1))
        code = slot | (pos << slot_bits)
        before = waiting[which * blocks + place]
        end = waiting[2 * kinds * blocks + which]
        plan_ref[which * entries + end] = pair(place, before, code)
        waiting[which * blocks + place] = jnp.where(before >= 0, -1, code)
        waiting[2 * kinds * blocks + which] = end + (before >= 0).astype(jnp.int32)
        return carry

    lax.fori_loop(0, count_ref[0, 0], turn, 0)
    for which in range(2 * kinds):
        end = waiting[2 * kinds * blocks + which]
        for place in range(places_of(which, blocks_dev)):
            before = waiting[which * blocks + place]
            plan_ref[which * entries + end] = pair(place, before, empty)
            end = end + (before >= 0).astype(jnp.int32)
        for extra in range(unroll):
            plan_ref[which * entries + end + extra] = pair(0, empty, empty)
        plan_ref[2 * kinds * entries + which] = end


def pack(half, *refs):
    first, second = refs[:side], refs[side : 2 * side]
    notes_from = refs[2 * side : 4 * side - 2]
    outs = refs[4 * side - 2 : 6 * side - 4]
    notes, sems = refs[6 * side - 4 :]
    rows = side * half
    copies = [
        pltpu.make_async_copy(
            source.at[rows : rows + note_rows, :lanes], notes.at[at], sems.at[at]
        )
        for at, source in enumerate(notes_from)
    ]
    for copy in copies:
        copy.start()
    for copy in copies:
        copy.wait()
    my_z = lax.axis_index("row") // side
    my_y = lax.axis_index("row") % side
    for away in range(1, side):
        for d in range(side):
            next_y = lax.rem(my_y + d, side)
            next_z = lax.rem(my_z + d, side)
            for j in range(picks):
                spot = spot_of(d, j, half)
                along_z = notes[away - 1, j, my_z * side + next_y].astype(jnp.int32)
                outs[away - 1][spot, :] = first[d][half_at(along_z, half), :]
                along_y = notes[side + away - 2, j, next_z * side + my_y].astype(jnp.int32)
                outs[side + away - 2][spot, :] = second[d][half_at(along_y, half), :]


def pack_group(first, second, notes, half):
    packed = jax.ShapeDtypeStruct((side * picks * half, span), jnp.float32)
    number = 2 * (side - 1)
    return pl.pallas_call(
        lambda *refs: pack(half, *refs),
        in_specs=[in_vmem] * (2 * side + number),
        out_specs=[in_vmem] * number,
        scratch_shapes=[
            pltpu.SMEM((number, note_rows, lanes), jnp.float32),
            pltpu.SemaphoreType.DMA((number,)),
        ],
        out_shape=[packed] * number,
        compiler_params=pltpu.CompilerParams(vmem_limit_bytes=5 << 20),
        cost_estimate=pl.CostEstimate(flops=0, bytes_accessed=5 << 20, transcendentals=0),
        name="pack",
    )(*first, *second, *notes)


def add_tiles(which, blocks_dev, plan_ref, tile_ref, pool, total):
    tile_total = tile_ref.shape[0]
    sources = pool.shape[0] - 1
    entries = pairs_of(tile_total, blocks_dev)
    slot_bits = log(tile_total)
    pos_bits = log(sources) + 1
    total[...] = jnp.zeros_like(total)

    def turn(step, carry):
        products = []
        for lane in range(unroll):
            code = plan_ref[which * entries + step * unroll + lane]
            left, right = [], []
            for _ in range(2):
                left.append(tile_ref[code & (tile_total - 1)].astype(jnp.bfloat16))
                code = lax.shift_right_logical(code, slot_bits)
                right.append(pool[code & ((1 << pos_bits) - 1)])
                code = lax.shift_right_logical(code, pos_bits)
            product = jnp.dot(
                jnp.concatenate(left, axis=1),
                jnp.concatenate(right, axis=0),
                preferred_element_type=jnp.float32,
            )
            products.append((code, product))
        for target, product in products:
            total[target] += product
        return carry

    count = plan_ref[2 * kinds * entries + which]
    lax.fori_loop(0, (count + unroll - 1) // unroll, turn, 0)


def combine(blocks_dev, plan_ref, need_ref, tile_ref, *refs):
    first, second = refs[:side], refs[side : 2 * side]
    along_z = refs[2 * side : 3 * side - 1]
    along_y = refs[3 * side - 1 : 4 * side - 2]
    total, pool = refs[4 * side - 2 :]
    half = pool.shape[1] // 2
    top, low = slice(0, half), slice(half, 2 * half)
    my_z = lax.axis_index("row") // side
    my_y = lax.axis_index("row") % side
    for d in range(side):
        next_y = lax.rem(my_y + d, side)
        next_z = lax.rem(my_z + d, side)
        for j in range(picks):
            mine = need_ref[j, my_z * side + next_y]
            pool[d * picks + j, top, :] = first[d][half_at(mine, half), :].astype(pool.dtype)
            mine = need_ref[j, next_z * side + my_y]
            pool[d * side * picks + j, low, :] = second[d][half_at(mine, half), :].astype(
                pool.dtype
            )
            spot = spot_of(d, j, half)
            for away in range(1, side):
                pool[(back(away) * side + d) * picks + j, top, :] = along_z[away - 1][
                    spot, :
                ].astype(pool.dtype)
                pool[(d * side + back(away)) * picks + j, low, :] = along_y[away - 1][
                    spot, :
                ].astype(pool.dtype)
    pool[side * side * picks] = jnp.zeros(pool.shape[1:], pool.dtype)
    add_tiles(0, blocks_dev, plan_ref, tile_ref, pool, total)


def combine_sent(listed, need, tiles, first, second, along_z, along_y, blocks_dev):
    edge = tiles.shape[1]
    return pl.pallas_call(
        lambda *refs: combine(blocks_dev, *refs),
        in_specs=[in_smem] * 2 + [in_vmem] * (4 * side - 1),
        out_specs=[in_vmem] * 2,
        out_shape=[
            jax.ShapeDtypeStruct((places_of(0, blocks_dev), edge, span), jnp.float32),
            jax.ShapeDtypeStruct((side * side * picks + 1, edge, span), jnp.bfloat16),
        ],
        compiler_params=pltpu.CompilerParams(vmem_limit_bytes=10 << 20),
        cost_estimate=pl.CostEstimate(flops=2 << 30, bytes_accessed=10 << 20, transcendentals=0),
        name="combine",
    )(listed, need, tiles, *first, *second, *along_z, *along_y)


def combine_listed(which, listed, tiles, pool, blocks_dev):
    edge = tiles.shape[1]
    return pl.pallas_call(
        lambda *refs: add_tiles(which, blocks_dev, *refs),
        in_specs=[in_smem] + [in_vmem] * 2,
        out_specs=in_vmem,
        out_shape=jax.ShapeDtypeStruct((places_of(which, blocks_dev), edge, span), jnp.float32),
        compiler_params=pltpu.CompilerParams(vmem_limit_bytes=6 << 20),
        cost_estimate=pl.CostEstimate(flops=2 << 30, bytes_accessed=8 << 20, transcendentals=0),
        name="listed",
    )(listed, tiles, pool)


def mix(group, feature_ref, totals, mixed):
    part = slice(group * span, (group + 1) * span)
    (mine, other), rest = totals[:2], totals[2:]
    rows = rest[0].shape[0]
    for at in range(2):
        spot = slice(at * rows, (at + 1) * rows)
        summed = mine[spot, :] + other[spot, :] + rest[2 * at][...] + rest[2 * at + 1][...]
        mixed[spot, :] = ((1.0 + gin_epsilon) * feature_ref[spot, part] + summed).astype(mixed.dtype)


def begin_mlp(feature_ref, w_ref, bias_ref, *refs):
    totals, (out_ref, mixed) = refs[:-2], refs[-2:]
    mix(0, feature_ref, totals, mixed)

    def turn(step, carry):
        part = pl.ds(pl.multiple_of(step * chunk, chunk), chunk)
        out_ref[part, :] = (
            jnp.dot(mixed[part, :], w_ref[:span, :], preferred_element_type=jnp.float32)
            + bias_ref[...]
        )
        return carry

    lax.fori_loop(0, out_ref.shape[0] // chunk, turn, 0)


def end_mlp(feature_ref, w_ref, before_ref, w_out_ref, bias_ref, *refs):
    totals, (out_ref, mixed) = refs[:-2], refs[-2:]
    mix(1, feature_ref, totals, mixed)

    def turn(step, carry):
        part = pl.ds(pl.multiple_of(step * chunk, chunk), chunk)
        hidden = before_ref[part, :] + jnp.dot(
            mixed[part, :], w_ref[span:, :], preferred_element_type=jnp.float32
        )
        hidden = jnp.maximum(hidden, 0.0).astype(jnp.bfloat16)
        updated = jnp.dot(hidden, w_out_ref[...], preferred_element_type=jnp.float32)
        out_ref[part, :] = (updated + bias_ref[...]).astype(out_ref.dtype)
        return carry

    lax.fori_loop(0, out_ref.shape[0] // chunk, turn, 0)


def on_device(
    features, tiles, tile_rows, tile_cols, tile_count, needed, w_in, bias_in, w_out, bias_out
):
    edge = tiles.shape[-1]
    half = edge // 2
    nodes, width = features.shape
    blocks_dev = nodes // edge
    hidden_size = w_in.shape[1]
    blocks = places_of(1, blocks_dev)
    groups = width // span

    need = needed[0, 0].T
    firsts, seconds = [], []
    for group in range(groups):
        top, low = split_group(group, features, need)
        first = [top] + [None] * (side - 1)
        second = [low] + [None] * (side - 1)
        for away in (1, 3, 2):
            first[away] = from_y(first[0], away)
            second[away] = from_z(second[0], away)
        firsts.append(first)
        seconds.append(second)
    notes = seconds[0][1:] + firsts[0][1:]

    listed = pl.pallas_call(
        lambda *refs: plan(*refs, blocks_dev),
        in_specs=[in_smem] * 3,
        out_specs=in_smem,
        out_shape=jax.ShapeDtypeStruct((512,), jnp.int32),
        scratch_shapes=[pltpu.SMEM((2 * kinds * (blocks + 1),), jnp.int32)],
        compiler_params=pltpu.CompilerParams(vmem_limit_bytes=1 << 20),
        cost_estimate=pl.CostEstimate(flops=0, bytes_accessed=1 << 20, transcendentals=0),
        name="plan",
    )(tile_rows[0, 0], tile_cols[0, 0], tile_count)
    cell_tiles = tiles[0, 0]

    sums = []
    for group in range(groups):
        first, second = firsts[group], seconds[group]
        packed = pack_group(first, second, notes, half)
        along_z, along_y = [None] * (side - 1), [None] * (side - 1)
        for away in (1, 3, 2):
            along_z[away - 1] = from_z(packed[away - 1], -away)
            along_y[away - 1] = from_y(packed[side + away - 2], -away)
        send, pool = combine_sent(
            listed, need, cell_tiles, first, second, along_z, along_y, blocks_dev
        )
        arrived = lax.ppermute(send, "col", col_shift(0, 1))
        keep = combine_listed(kinds, listed, cell_tiles, pool, blocks_dev)
        over_right, over_left = pl.pallas_call(
            join_across,
            in_specs=[in_vmem] * 2,
            out_specs=[in_vmem] * 2,
            out_shape=[jax.ShapeDtypeStruct((blocks_dev // 2, edge, span), jnp.float32)] * 2,
            compiler_params=pltpu.CompilerParams(vmem_limit_bytes=4 << 20),
            cost_estimate=pl.CostEstimate(flops=0, bytes_accessed=2 << 20, transcendentals=0),
            name="join",
        )(keep, arrived)
        relay_right = lax.ppermute(over_right, "col", col_shift(1, 0))
        relay_left = lax.ppermute(over_left, "col", col_shift(-1, 0))
        send = combine_listed(1, listed, cell_tiles, pool, blocks_dev)
        arrived = lax.ppermute(send, "col", col_shift(0, 1))
        keep = combine_listed(kinds + 1, listed, cell_tiles, pool, blocks_dev)
        cut = blocks_dev // 2
        right_held, right, left, left_held = pl.pallas_call(
            join_rest,
            in_specs=[in_vmem] * 2,
            out_specs=[in_vmem] * 4,
            out_shape=[jax.ShapeDtypeStruct((cut, edge, span), jnp.float32)] * 4,
            compiler_params=pltpu.CompilerParams(vmem_limit_bytes=6 << 20),
            cost_estimate=pl.CostEstimate(flops=0, bytes_accessed=4 << 20, transcendentals=0),
            name="join",
        )(keep, arrived)
        from_left = lax.ppermute(right, "col", col_shift(1, 0))
        from_right = lax.ppermute(left, "col", col_shift(-1, 0))
        right_held, left_held = pl.pallas_call(
            relay,
            in_specs=[in_vmem] * 4,
            out_specs=[in_vmem] * 2,
            out_shape=[jax.ShapeDtypeStruct((cut, edge, span), jnp.float32)] * 2,
            compiler_params=pltpu.CompilerParams(vmem_limit_bytes=4 << 20),
            cost_estimate=pl.CostEstimate(flops=0, bytes_accessed=2 << 20, transcendentals=0),
            name="relay",
        )(right_held, left_held, relay_right, relay_left)
        from_left_held = lax.ppermute(right_held, "col", col_shift(1, 0))
        from_right_held = lax.ppermute(left_held, "col", col_shift(-1, 0))
        send = combine_listed(2, listed, cell_tiles, pool, blocks_dev)
        arrived = lax.ppermute(send, "col", col_shift(0, 1))
        keep = combine_listed(kinds + 2, listed, cell_tiles, pool, blocks_dev)
        sums.append(
            [
                v.reshape(-1, span)
                for v in (
                    keep,
                    arrived,
                    from_left_held,
                    from_right,
                    from_left,
                    from_right_held,
                )
            ]
        )

    before = pl.pallas_call(
        begin_mlp,
        in_specs=[in_vmem] * (3 + len(sums[0])),
        out_specs=in_vmem,
        out_shape=jax.ShapeDtypeStruct((nodes, hidden_size), jnp.float32),
        scratch_shapes=[pltpu.VMEM((nodes, span), jnp.bfloat16)],
        compiler_params=pltpu.CompilerParams(vmem_limit_bytes=8 << 20),
        cost_estimate=pl.CostEstimate(
            flops=1 << 29, bytes_accessed=8 << 20, transcendentals=0
        ),
        name="begin",
    )(features, w_in, bias_in.reshape(1, -1), *sums[0])
    return pl.pallas_call(
        end_mlp,
        in_specs=[in_vmem] * (5 + len(sums[1])),
        out_specs=in_vmem,
        out_shape=jax.ShapeDtypeStruct((nodes, width), jnp.bfloat16),
        scratch_shapes=[pltpu.VMEM((nodes, span), jnp.bfloat16)],
        compiler_params=pltpu.CompilerParams(vmem_limit_bytes=8 << 20),
        cost_estimate=pl.CostEstimate(
            flops=3 << 29, bytes_accessed=8 << 20, transcendentals=0
        ),
        name="end",
    )(features, w_in, before, w_out, bias_out.reshape(1, -1), *sums[1])


def solution(mesh):
    placed = (
        P(("row", "col"), None),
        P("row", "col", None, None, None),
        P("row", "col", None),
        P("row", "col", None),
        P("row", "col"),
        P("row", "col", None, None),
        P(),
        P(),
        P(),
        P(),
    )

    return jax.shard_map(
        on_device, mesh=mesh, in_specs=placed, out_specs=P(("row", "col"), None), check_vma=False
    )
```

```python
import jax
import jax.numpy as jnp
from jax import lax
from jax.experimental import pallas as pl
from jax.experimental.pallas import tpu as pltpu
from jax.sharding import PartitionSpec as P


gin_epsilon = 0.25
unroll = 8
span = 256
side = 4
cores = 2
picks = 2
kinds = 3
across_x = side // 2
note_rows = 8
lanes = 128
chunk = 256

in_vmem = pl.BlockSpec(memory_space=pltpu.VMEM)
in_smem = pl.BlockSpec(memory_space=pltpu.SMEM)


def row_shift(step_z, step_y):
    return [
        (z * side + y, (z + step_z) % side * side + (y + step_y) % side)
        for z in range(side)
        for y in range(side)
    ]


def col_shift(step_x, step_core):
    return [
        (x * cores + k, (x + step_x) % side * cores + (k + step_core) % cores)
        for x in range(side)
        for k in range(cores)
    ]


def from_z(value, step):
    return lax.ppermute(value, "row", row_shift(-step, 0))


def from_y(value, step):
    return lax.ppermute(value, "row", row_shift(0, -step))


def back(step):
    return (side - step) % side


def half_at(number, half):
    return pl.ds(pl.multiple_of(number * half, half), half)


def spot_of(d, j, half):
    return slice((d * picks + j) * half, (d * picks + j + 1) * half)


def split(group, feature_ref, *refs):
    noted = group == 0
    if noted:
        need_ref, first_ref, second_ref, need, sems = refs
    else:
        first_ref, second_ref, sems = refs
    half = lanes // 2
    rows = feature_ref.shape[0] // 2
    part = slice(group * span, (group + 1) * span)
    copies = []
    for place, out in enumerate((first_ref, second_ref)):
        for block in range(rows // half):
            start = (2 * block + place) * half
            copies.append(
                pltpu.make_async_copy(
                    feature_ref.at[start : start + half, part],
                    out.at[block * half : (block + 1) * half, :],
                    sems.at[len(copies)],
                )
            )
    if noted:
        copy = pltpu.make_async_copy(need_ref, need, sems.at[len(copies)])
        copy.start()
    for each in copies:
        each.start()
    if noted:
        copy.wait()
        note = need[...].astype(jnp.float32)
        for out in (first_ref, second_ref):
            out[rows:, :] = jnp.zeros((note_rows, span), jnp.float32)
            out[rows : rows + note.shape[0], : note.shape[1]] = note
    for each in copies:
        each.wait()


def split_group(group, features, need):
    nodes = features.shape[0]
    args = [features] + ([need] if group == 0 else [])
    rows = nodes // 2 + (note_rows if group == 0 else 0)
    copies = nodes // lanes * 2 + (1 if group == 0 else 0)
    return pl.pallas_call(
        lambda *refs: split(group, *refs),
        in_specs=[pl.BlockSpec(memory_space=pltpu.HBM)] * len(args),
        out_specs=[in_vmem] * 2,
        scratch_shapes=([pltpu.VMEM(need.shape, jnp.int32)] if group == 0 else [])
        + [pltpu.SemaphoreType.DMA((copies,))],
        out_shape=[jax.ShapeDtypeStruct((rows, span), jnp.float32)] * 2,
        compiler_params=pltpu.CompilerParams(vmem_limit_bytes=4 << 20),
        cost_estimate=pl.CostEstimate(flops=0, bytes_accessed=1 << 20, transcendentals=0),
        name="split",
    )(*[pltpu.with_memory_space_constraint(v, pltpu.HBM) for v in args])


def join_across(keep_ref, arrived_ref, over_right_ref, over_left_ref):
    cut = over_right_ref.shape[0]
    over_right_ref[...] = keep_ref[:cut] + arrived_ref[:cut]
    over_left_ref[...] = keep_ref[cut:] + arrived_ref[cut:]


def join_rest(keep_ref, arrived_ref, *outs):
    start = 0
    for out in outs:
        spot = slice(start, start + out.shape[0])
        out[...] = keep_ref[spot] + arrived_ref[spot]
        start = spot.stop


def relay(from_left_ref, from_right_ref, *refs):
    helds, outs = refs[: len(refs) // 2], refs[len(refs) // 2 :]
    pieces = len(outs) // 2
    for at, (held, out) in enumerate(zip(helds, outs)):
        size = out.shape[0]
        source = from_left_ref if at < pieces else from_right_ref
        start = at % pieces * size
        out[...] = held[...] + source[start : start + size]


def log(value):
    return value.bit_length() - 1


def places_of(which, blocks_dev):
    return blocks_dev * (2 if which % kinds == 1 else 1)


def pairs_of(tile_total, blocks_dev):
    return (tile_total + places_of(1, blocks_dev)) // 2 + unroll


def plan(row_ref, col_ref, count_ref, plan_ref, waiting, blocks_dev):
    tile_total = row_ref.shape[0]
    blocks = places_of(1, blocks_dev)
    entries = pairs_of(tile_total, blocks_dev)
    slot_bits = log(tile_total)
    code_bits = slot_bits + log(side * side * picks) + 1
    empty = (side * side * picks) << slot_bits
    my_z = lax.axis_index("row") // side
    my_y = lax.axis_index("row") % side
    my_x = lax.axis_index("col") // cores
    my_core = lax.axis_index("col") % cores

    def pair(place, first, second):
        return first | (second << code_bits) | (place << (2 * code_bits))

    for place in range(2 * kinds * blocks):
        waiting[place] = -1
    for which in range(2 * kinds):
        waiting[2 * kinds * blocks + which] = 0

    def turn(slot, carry):
        target = row_ref[slot]
        source = col_ref[slot]
        column = lax.shift_right_logical(target, log(blocks_dev))
        away_x = (lax.shift_right_logical(column, log(cores)) - my_x) & (side - 1)
        beside = away_x & 1
        kind = jnp.where(beside == 1, 1, jnp.where(away_x == across_x, 0, 2))
        right = (away_x > across_x).astype(jnp.int32)
        place = right * blocks_dev + (target & (blocks_dev - 1))
        which = kinds * (1 - ((column & (cores - 1)) ^ my_core)) + kind
        owner = lax.shift_right_logical(source, log(picks))
        away_z = (lax.shift_right_logical(owner, log(side)) - my_z) & (side - 1)
        away_y = (owner - my_y) & (side - 1)
        pos = (away_z * side + away_y) * picks + (source & (picks - 1))
        code = slot | (pos << slot_bits)
        before = waiting[which * blocks + place]
        end = waiting[2 * kinds * blocks + which]
        plan_ref[which * entries + end] = pair(place, before, code)
        waiting[which * blocks + place] = jnp.where(before >= 0, -1, code)
        waiting[2 * kinds * blocks + which] = end + (before >= 0).astype(jnp.int32)
        return carry

    lax.fori_loop(0, count_ref[0, 0], turn, 0)
    for which in range(2 * kinds):
        end = waiting[2 * kinds * blocks + which]
        for place in range(places_of(which, blocks_dev)):
            before = waiting[which * blocks + place]
            plan_ref[which * entries + end] = pair(place, before, empty)
            end = end + (before >= 0).astype(jnp.int32)
        for extra in range(unroll):
            plan_ref[which * entries + end + extra] = pair(0, empty, empty)
        plan_ref[2 * kinds * entries + which] = end


def pack(half, *refs):
    first, second = refs[:side], refs[side : 2 * side]
    notes_from = refs[2 * side : 4 * side - 2]
    outs = refs[4 * side - 2 : 6 * side - 4]
    notes, sems = refs[6 * side - 4 :]
    rows = side * half
    copies = [
        pltpu.make_async_copy(
            source.at[rows : rows + note_rows, :lanes], notes.at[at], sems.at[at]
        )
        for at, source in enumerate(notes_from)
    ]
    for copy in copies:
        copy.start()
    for copy in copies:
        copy.wait()
    my_z = lax.axis_index("row") // side
    my_y = lax.axis_index("row") % side
    for away in range(1, side):
        for d in range(side):
            next_y = lax.rem(my_y + d, side)
            next_z = lax.rem(my_z + d, side)
            for j in range(picks):
                spot = spot_of(d, j, half)
                along_z = notes[away - 1, j, my_z * side + next_y].astype(jnp.int32)
                outs[away - 1][spot, :] = first[d][half_at(along_z, half), :]
                along_y = notes[side + away - 2, j, next_z * side + my_y].astype(jnp.int32)
                outs[side + away - 2][spot, :] = second[d][half_at(along_y, half), :]


def pack_group(first, second, notes, half):
    packed = jax.ShapeDtypeStruct((side * picks * half, span), jnp.float32)
    number = 2 * (side - 1)
    return pl.pallas_call(
        lambda *refs: pack(half, *refs),
        in_specs=[in_vmem] * (2 * side + number),
        out_specs=[in_vmem] * number,
        scratch_shapes=[
            pltpu.SMEM((number, note_rows, lanes), jnp.float32),
            pltpu.SemaphoreType.DMA((number,)),
        ],
        out_shape=[packed] * number,
        compiler_params=pltpu.CompilerParams(vmem_limit_bytes=5 << 20),
        cost_estimate=pl.CostEstimate(flops=0, bytes_accessed=5 << 20, transcendentals=0),
        name="pack",
    )(*first, *second, *notes)


def add_tiles(which, blocks_dev, plan_ref, tile_ref, pool, total):
    tile_total = tile_ref.shape[0]
    sources = pool.shape[0] - 1
    entries = pairs_of(tile_total, blocks_dev)
    slot_bits = log(tile_total)
    pos_bits = log(sources) + 1
    total[...] = jnp.zeros_like(total)

    def turn(step, carry):
        products = []
        for lane in range(unroll):
            code = plan_ref[which * entries + step * unroll + lane]
            left, right = [], []
            for _ in range(2):
                left.append(tile_ref[code & (tile_total - 1)].astype(jnp.bfloat16))
                code = lax.shift_right_logical(code, slot_bits)
                right.append(pool[code & ((1 << pos_bits) - 1)])
                code = lax.shift_right_logical(code, pos_bits)
            product = jnp.dot(
                jnp.concatenate(left, axis=1),
                jnp.concatenate(right, axis=0),
                preferred_element_type=jnp.float32,
            )
            products.append((code, product))
        for target, product in products:
            total[target] += product
        return carry

    count = plan_ref[2 * kinds * entries + which]
    lax.fori_loop(0, (count + unroll - 1) // unroll, turn, 0)


def combine(blocks_dev, plan_ref, need_ref, tile_ref, *refs):
    first, second = refs[:side], refs[side : 2 * side]
    along_z = refs[2 * side : 3 * side - 1]
    along_y = refs[3 * side - 1 : 4 * side - 2]
    total, pool = refs[4 * side - 2 :]
    half = pool.shape[1] // 2
    top, low = slice(0, half), slice(half, 2 * half)
    my_z = lax.axis_index("row") // side
    my_y = lax.axis_index("row") % side
    for d in range(side):
        next_y = lax.rem(my_y + d, side)
        next_z = lax.rem(my_z + d, side)
        for j in range(picks):
            mine = need_ref[j, my_z * side + next_y]
            pool[d * picks + j, top, :] = first[d][half_at(mine, half), :].astype(pool.dtype)
            mine = need_ref[j, next_z * side + my_y]
            pool[d * side * picks + j, low, :] = second[d][half_at(mine, half), :].astype(
                pool.dtype
            )
            spot = spot_of(d, j, half)
            for away in range(1, side):
                pool[(back(away) * side + d) * picks + j, top, :] = along_z[away - 1][
                    spot, :
                ].astype(pool.dtype)
                pool[(d * side + back(away)) * picks + j, low, :] = along_y[away - 1][
                    spot, :
                ].astype(pool.dtype)
    pool[side * side * picks] = jnp.zeros(pool.shape[1:], pool.dtype)
    add_tiles(0, blocks_dev, plan_ref, tile_ref, pool, total)


def combine_sent(listed, need, tiles, first, second, along_z, along_y, blocks_dev):
    edge = tiles.shape[1]
    return pl.pallas_call(
        lambda *refs: combine(blocks_dev, *refs),
        in_specs=[in_smem] * 2 + [in_vmem] * (4 * side - 1),
        out_specs=[in_vmem] * 2,
        out_shape=[
            jax.ShapeDtypeStruct((places_of(0, blocks_dev), edge, span), jnp.float32),
            jax.ShapeDtypeStruct((side * side * picks + 1, edge, span), jnp.bfloat16),
        ],
        compiler_params=pltpu.CompilerParams(vmem_limit_bytes=10 << 20),
        cost_estimate=pl.CostEstimate(flops=2 << 30, bytes_accessed=10 << 20, transcendentals=0),
        name="combine",
    )(listed, need, tiles, *first, *second, *along_z, *along_y)


def combine_listed(which_ones, listed, tiles, pool, blocks_dev):
    edge = tiles.shape[1]

    def body(plan_ref, tile_ref, pool_ref, *totals):
        for which, total in zip(which_ones, totals):
            add_tiles(which, blocks_dev, plan_ref, tile_ref, pool_ref, total)

    return pl.pallas_call(
        body,
        in_specs=[in_smem] + [in_vmem] * 2,
        out_specs=[in_vmem] * len(which_ones),
        out_shape=[
            jax.ShapeDtypeStruct((places_of(which, blocks_dev), edge, span), jnp.float32)
            for which in which_ones
        ],
        compiler_params=pltpu.CompilerParams(vmem_limit_bytes=6 << 20),
        cost_estimate=pl.CostEstimate(flops=2 << 30, bytes_accessed=8 << 20, transcendentals=0),
        name="listed",
    )(listed, tiles, pool)


def mix(group, feature_ref, keep, arrived, from_right, from_left, left_held, right_held, piece):
    part = slice(group * span, (group + 1) * span)
    pieces = keep.shape[0] // lanes // 2
    shift = 0 if left_held.shape[0] > lanes else piece
    whole = slice(piece * lanes, (piece + 1) * lanes)
    own = slice((piece - shift) * lanes, (piece - shift + 1) * lanes)
    mixed = []
    for low, ready, held in ((0, from_right, left_held), (1, from_left, right_held)):
        spot = slice((low * pieces + piece) * lanes, (low * pieces + piece + 1) * lanes)
        summed = keep[spot, :] + arrived[spot, :] + ready[whole, :] + held[own, :]
        mixed.append(((1.0 + gin_epsilon) * feature_ref[spot, part] + summed).astype(jnp.bfloat16))
    return mixed


def begin_mlp(feature_ref, w_ref, bias_ref, *refs):
    totals, (out_ref, mixed) = refs[:-2], refs[-2:]
    for piece in range(mixed.shape[0] // lanes // 2):
        for low, value in enumerate(mix(0, feature_ref, *totals, piece)):
            mixed[(2 * piece + low) * lanes : (2 * piece + low + 1) * lanes, :] = value

    def turn(step, carry):
        part = pl.ds(pl.multiple_of(step * chunk, chunk), chunk)
        out_ref[part, :] = (
            jnp.dot(mixed[part, :], w_ref[:span, :], preferred_element_type=jnp.float32)
            + bias_ref[...]
        )
        return carry

    lax.fori_loop(0, out_ref.shape[0] // chunk, turn, 0)


def end_mlp(piece, feature_ref, w_ref, before_ref, w_out_ref, bias_ref, *refs):
    totals, (out_ref, mixed, result, sems) = refs[:6], refs[-4:]
    for low, value in enumerate(mix(1, feature_ref, *totals, piece)):
        mixed[low * lanes : (low + 1) * lanes, :] = value
    rows = mixed.shape[0]
    hidden = before_ref[piece * rows : (piece + 1) * rows, :] + jnp.dot(
        mixed[...], w_ref[span:, :], preferred_element_type=jnp.float32
    )
    hidden = jnp.maximum(hidden, 0.0).astype(jnp.bfloat16)
    updated = jnp.dot(hidden, w_out_ref[...], preferred_element_type=jnp.float32)
    result[...] = (updated + bias_ref[...]).astype(result.dtype)
    pieces = out_ref.shape[0] // rows
    copies = [
        pltpu.make_async_copy(
            result.at[low * lanes : (low + 1) * lanes, :],
            out_ref.at[(low * pieces + piece) * lanes : (low * pieces + piece + 1) * lanes, :],
            sems.at[low],
        )
        for low in range(2)
    ]
    for copy in copies:
        copy.start()
    for copy in copies:
        copy.wait()


def on_device(
    features, tiles, tile_rows, tile_cols, tile_count, needed, w_in, bias_in, w_out, bias_out
):
    edge = tiles.shape[-1]
    half = edge // 2
    nodes, width = features.shape
    blocks_dev = nodes // edge
    hidden_size = w_in.shape[1]
    blocks = places_of(1, blocks_dev)
    groups = width // span

    need = needed[0, 0].T
    firsts, seconds = [], []
    for group in range(groups):
        top, low = split_group(group, features, need)
        first = [top] + [None] * (side - 1)
        second = [low] + [None] * (side - 1)
        for away in (1, 3, 2):
            first[away] = from_y(first[0], away)
            second[away] = from_z(second[0], away)
        firsts.append(first)
        seconds.append(second)
    notes = seconds[0][1:] + firsts[0][1:]

    listed = pl.pallas_call(
        lambda *refs: plan(*refs, blocks_dev),
        in_specs=[in_smem] * 3,
        out_specs=in_smem,
        out_shape=jax.ShapeDtypeStruct((512,), jnp.int32),
        scratch_shapes=[pltpu.SMEM((2 * kinds * (blocks + 1),), jnp.int32)],
        compiler_params=pltpu.CompilerParams(vmem_limit_bytes=1 << 20),
        cost_estimate=pl.CostEstimate(flops=0, bytes_accessed=1 << 20, transcendentals=0),
        name="plan",
    )(tile_rows[0, 0], tile_cols[0, 0], tile_count)
    cell_tiles = tiles[0, 0]

    sums = []
    for group in range(groups):
        first, second = firsts[group], seconds[group]
        packed = pack_group(first, second, notes, half)
        along_z, along_y = [None] * (side - 1), [None] * (side - 1)
        for away in (1, 3, 2):
            along_z[away - 1] = from_z(packed[away - 1], -away)
            along_y[away - 1] = from_y(packed[side + away - 2], -away)
        send, pool = combine_sent(
            listed, need, cell_tiles, first, second, along_z, along_y, blocks_dev
        )
        arrived = lax.ppermute(send, "col", col_shift(0, 1))
        keep, sides = combine_listed((kinds, 1), listed, cell_tiles, pool, blocks_dev)
        over_right, over_left = pl.pallas_call(
            join_across,
            in_specs=[in_vmem] * 2,
            out_specs=[in_vmem] * 2,
            out_shape=[jax.ShapeDtypeStruct((blocks_dev // 2, edge, span), jnp.float32)] * 2,
            compiler_params=pltpu.CompilerParams(vmem_limit_bytes=4 << 20),
            cost_estimate=pl.CostEstimate(flops=0, bytes_accessed=2 << 20, transcendentals=0),
            name="join",
        )(keep, arrived)
        relay_right = lax.ppermute(over_right, "col", col_shift(1, 0))
        relay_left = lax.ppermute(over_left, "col", col_shift(-1, 0))
        arrived = lax.ppermute(sides, "col", col_shift(0, 1))
        keep, mine_sent, mine_kept = combine_listed(
            (kinds + 1, 2, kinds + 2), listed, cell_tiles, pool, blocks_dev
        )
        cut = blocks_dev // 2
        held = [cut] if group < groups - 1 else [1] * cut
        sizes = held + [cut, cut] + held
        joined = pl.pallas_call(
            join_rest,
            in_specs=[in_vmem] * 2,
            out_specs=[in_vmem] * len(sizes),
            out_shape=[jax.ShapeDtypeStruct((n, edge, span), jnp.float32) for n in sizes],
            compiler_params=pltpu.CompilerParams(vmem_limit_bytes=6 << 20),
            cost_estimate=pl.CostEstimate(flops=0, bytes_accessed=4 << 20, transcendentals=0),
            name="join",
        )(keep, arrived)
        right_held, (right, left) = joined[: len(held)], joined[len(held) : len(held) + 2]
        left_held = joined[len(held) + 2 :]
        from_left = lax.ppermute(right, "col", col_shift(1, 0))
        from_right = lax.ppermute(left, "col", col_shift(-1, 0))
        relayed = pl.pallas_call(
            relay,
            in_specs=[in_vmem] * (2 + 2 * len(held)),
            out_specs=[in_vmem] * (2 * len(held)),
            out_shape=[jax.ShapeDtypeStruct((n, edge, span), jnp.float32) for n in held * 2],
            compiler_params=pltpu.CompilerParams(vmem_limit_bytes=4 << 20),
            cost_estimate=pl.CostEstimate(flops=0, bytes_accessed=2 << 20, transcendentals=0),
            name="relay",
        )(relay_right, relay_left, *right_held, *left_held)
        from_left_held, from_right_held = [], []
        for piece in range(len(held)):
            from_left_held.append(
                lax.ppermute(relayed[piece], "col", col_shift(1, 0))
            )
            from_right_held.append(
                lax.ppermute(relayed[len(held) + piece], "col", col_shift(-1, 0))
            )
        arrived = lax.ppermute(mine_sent, "col", col_shift(0, 1))
        sums.append((mine_kept, arrived, from_right, from_left, from_left_held, from_right_held))

    flat = [[jax.tree.map(lambda v: v.reshape(-1, span), part) for part in one] for one in sums]
    *ready, (left_part,), (right_part,) = flat[0]
    before = pl.pallas_call(
        begin_mlp,
        in_specs=[in_vmem] * 9,
        out_specs=in_vmem,
        out_shape=jax.ShapeDtypeStruct((nodes, hidden_size), jnp.float32),
        scratch_shapes=[pltpu.VMEM((nodes, span), jnp.bfloat16)],
        compiler_params=pltpu.CompilerParams(vmem_limit_bytes=8 << 20),
        cost_estimate=pl.CostEstimate(
            flops=1 << 29, bytes_accessed=8 << 20, transcendentals=0
        ),
        name="begin",
    )(features, w_in, bias_in.reshape(1, -1), *ready, left_part, right_part)
    updated = []
    *ready, left_parts, right_parts = flat[1]
    for piece in range(len(left_parts)):
        rows = nodes // len(left_parts)
        hbm = pl.BlockSpec(memory_space=pltpu.HBM)
        updated = [
            pl.pallas_call(
                lambda *refs: end_mlp(piece, *refs),
                in_specs=[in_vmem] * 11 + [hbm] * len(updated),
                out_specs=hbm,
                out_shape=jax.ShapeDtypeStruct((nodes, width), jnp.bfloat16),
                scratch_shapes=[
                    pltpu.VMEM((rows, span), jnp.bfloat16),
                    pltpu.VMEM((rows, width), jnp.bfloat16),
                    pltpu.SemaphoreType.DMA((2,)),
                ],
                input_output_aliases={11: 0} if updated else {},
                compiler_params=pltpu.CompilerParams(vmem_limit_bytes=8 << 20),
                cost_estimate=pl.CostEstimate(
                    flops=3 << 28, bytes_accessed=4 << 20, transcendentals=0
                ),
                name="end",
            )(
                features,
                w_in,
                before,
                w_out,
                bias_out.reshape(1, -1),
                *ready,
                left_parts[piece],
                right_parts[piece],
                *updated,
            )
        ]
    return updated[0]


def solution(mesh):
    placed = (
        P(("row", "col"), None),
        P("row", "col", None, None, None),
        P("row", "col", None),
        P("row", "col", None),
        P("row", "col"),
        P("row", "col", None, None),
        P(),
        P(),
        P(),
        P(),
    )

    return jax.shard_map(
        on_device, mesh=mesh, in_specs=placed, out_specs=P(("row", "col"), None), check_vma=False
    )
```

```python
import jax
import jax.numpy as jnp
from jax import lax
from jax.experimental import pallas as pl
from jax.experimental.pallas import tpu as pltpu
from jax.sharding import PartitionSpec as P


gin_epsilon = 0.25
unroll = 8
span = 256
side = 4
cores = 2
picks = 2
kinds = 3
across_x = side // 2
near = (1, 3)
note_rows = 8
lanes = 128
chunk = 256

in_vmem = pl.BlockSpec(memory_space=pltpu.VMEM)
in_smem = pl.BlockSpec(memory_space=pltpu.SMEM)


def row_shift(step_z, step_y):
    return [
        (z * side + y, (z + step_z) % side * side + (y + step_y) % side)
        for z in range(side)
        for y in range(side)
    ]


def col_shift(step_x, step_core):
    return [
        (x * cores + k, (x + step_x) % side * cores + (k + step_core) % cores)
        for x in range(side)
        for k in range(cores)
    ]


def from_z(value, step):
    return lax.ppermute(value, "row", row_shift(-step, 0))


def from_y(value, step):
    return lax.ppermute(value, "row", row_shift(0, -step))


def back(step):
    return (side - step) % side


def half_at(number, half):
    return pl.ds(pl.multiple_of(number * half, half), half)


def spot_of(d, j, half):
    return slice((d * picks + j) * half, (d * picks + j + 1) * half)


def split(group, feature_ref, *refs):
    noted = group == 0
    if noted:
        need_ref, first_ref, second_ref, need, sems = refs
    else:
        first_ref, second_ref, sems = refs
    half = lanes // 2
    rows = feature_ref.shape[0] // 2
    part = slice(group * span, (group + 1) * span)
    copies = []
    for place, out in enumerate((first_ref, second_ref)):
        for block in range(rows // half):
            start = (2 * block + place) * half
            copies.append(
                pltpu.make_async_copy(
                    feature_ref.at[start : start + half, part],
                    out.at[block * half : (block + 1) * half, :],
                    sems.at[len(copies)],
                )
            )
    if noted:
        copy = pltpu.make_async_copy(need_ref, need, sems.at[len(copies)])
        copy.start()
    for each in copies:
        each.start()
    if noted:
        copy.wait()
        note = need[...].astype(jnp.float32)
        for out in (first_ref, second_ref):
            out[rows:, :] = jnp.zeros((note_rows, span), jnp.float32)
            out[rows : rows + note.shape[0], : note.shape[1]] = note
    for each in copies:
        each.wait()


def split_group(group, features, need):
    nodes = features.shape[0]
    args = [features] + ([need] if group == 0 else [])
    rows = nodes // 2 + (note_rows if group == 0 else 0)
    copies = nodes // lanes * 2 + (1 if group == 0 else 0)
    return pl.pallas_call(
        lambda *refs: split(group, *refs),
        in_specs=[pl.BlockSpec(memory_space=pltpu.HBM)] * len(args),
        out_specs=[in_vmem] * 2,
        scratch_shapes=([pltpu.VMEM(need.shape, jnp.int32)] if group == 0 else [])
        + [pltpu.SemaphoreType.DMA((copies,))],
        out_shape=[jax.ShapeDtypeStruct((rows, span), jnp.float32)] * 2,
        compiler_params=pltpu.CompilerParams(vmem_limit_bytes=4 << 20),
        cost_estimate=pl.CostEstimate(flops=0, bytes_accessed=1 << 20, transcendentals=0),
        name="split",
    )(*[pltpu.with_memory_space_constraint(v, pltpu.HBM) for v in args])


def join_across(keep_ref, arrived_ref, over_right_ref, over_left_ref):
    cut = over_right_ref.shape[0]
    over_right_ref[...] = keep_ref[:cut] + arrived_ref[:cut]
    over_left_ref[...] = keep_ref[cut:] + arrived_ref[cut:]


def join_rest(keep_ref, arrived_ref, *outs):
    start = 0
    for out in outs:
        spot = slice(start, start + out.shape[0])
        out[...] = keep_ref[spot] + arrived_ref[spot]
        start = spot.stop


def relay(from_left_ref, from_right_ref, *refs):
    helds, outs = refs[: len(refs) // 2], refs[len(refs) // 2 :]
    pieces = len(outs) // 2
    for at, (held, out) in enumerate(zip(helds, outs)):
        size = out.shape[0]
        source = from_left_ref if at < pieces else from_right_ref
        start = at % pieces * size
        out[...] = held[...] + source[start : start + size]


def log(value):
    return value.bit_length() - 1


def places_of(which, blocks_dev):
    return blocks_dev * (2 if which % kinds == 1 else 1)


def pairs_of(tile_total, blocks_dev):
    return (tile_total + places_of(1, blocks_dev)) // 2 + unroll


def plan(row_ref, col_ref, count_ref, plan_ref, waiting, blocks_dev):
    tile_total = row_ref.shape[0]
    blocks = places_of(1, blocks_dev)
    entries = pairs_of(tile_total, blocks_dev)
    slot_bits = log(tile_total)
    code_bits = slot_bits + log(side * side * picks) + 1
    empty = (side * side * picks) << slot_bits
    my_z = lax.axis_index("row") // side
    my_y = lax.axis_index("row") % side
    my_x = lax.axis_index("col") // cores
    my_core = lax.axis_index("col") % cores

    def pair(place, first, second):
        return first | (second << code_bits) | (place << (2 * code_bits))

    for place in range(2 * kinds * blocks):
        waiting[place] = -1
    for which in range(2 * kinds):
        waiting[2 * kinds * blocks + which] = 0

    def turn(slot, carry):
        target = row_ref[slot]
        source = col_ref[slot]
        column = lax.shift_right_logical(target, log(blocks_dev))
        away_x = (lax.shift_right_logical(column, log(cores)) - my_x) & (side - 1)
        beside = away_x & 1
        kind = jnp.where(beside == 1, 1, jnp.where(away_x == across_x, 0, 2))
        right = (away_x > across_x).astype(jnp.int32)
        place = right * blocks_dev + (target & (blocks_dev - 1))
        which = kinds * (1 - ((column & (cores - 1)) ^ my_core)) + kind
        owner = lax.shift_right_logical(source, log(picks))
        away_z = (lax.shift_right_logical(owner, log(side)) - my_z) & (side - 1)
        away_y = (owner - my_y) & (side - 1)
        pos = (away_z * side + away_y) * picks + (source & (picks - 1))
        code = slot | (pos << slot_bits)
        before = waiting[which * blocks + place]
        end = waiting[2 * kinds * blocks + which]
        plan_ref[which * entries + end] = pair(place, before, code)
        waiting[which * blocks + place] = jnp.where(before >= 0, -1, code)
        waiting[2 * kinds * blocks + which] = end + (before >= 0).astype(jnp.int32)
        return carry

    lax.fori_loop(0, count_ref[0, 0], turn, 0)
    for which in range(2 * kinds):
        end = waiting[2 * kinds * blocks + which]
        for place in range(places_of(which, blocks_dev)):
            before = waiting[which * blocks + place]
            plan_ref[which * entries + end] = pair(place, before, empty)
            end = end + (before >= 0).astype(jnp.int32)
        for extra in range(unroll):
            plan_ref[which * entries + end + extra] = pair(0, empty, empty)
        plan_ref[2 * kinds * entries + which] = end


def pack(half, *refs):
    first, second = refs[:side], refs[side : 2 * side]
    notes_from = refs[2 * side : 4 * side - 2]
    outs = refs[4 * side - 2 : 6 * side - 4]
    notes, sems = refs[6 * side - 4 :]
    rows = side * half
    copies = [
        pltpu.make_async_copy(
            source.at[rows : rows + note_rows, :lanes], notes.at[at], sems.at[at]
        )
        for at, source in enumerate(notes_from)
    ]
    for copy in copies:
        copy.start()
    for copy in copies:
        copy.wait()
    my_z = lax.axis_index("row") // side
    my_y = lax.axis_index("row") % side
    for away in range(1, side):
        for d in range(side):
            next_y = lax.rem(my_y + d, side)
            next_z = lax.rem(my_z + d, side)
            for j in range(picks):
                spot = spot_of(d, j, half)
                along_z = notes[away - 1, j, my_z * side + next_y].astype(jnp.int32)
                outs[away - 1][spot, :] = first[d][half_at(along_z, half), :]
                along_y = notes[side + away - 2, j, next_z * side + my_y].astype(jnp.int32)
                outs[side + away - 2][spot, :] = second[d][half_at(along_y, half), :]


def pack_group(first, second, notes, half):
    packed = jax.ShapeDtypeStruct((side * picks * half, span), jnp.float32)
    number = 2 * (side - 1)
    return pl.pallas_call(
        lambda *refs: pack(half, *refs),
        in_specs=[in_vmem] * (2 * side + number),
        out_specs=[in_vmem] * number,
        scratch_shapes=[
            pltpu.SMEM((number, note_rows, lanes), jnp.float32),
            pltpu.SemaphoreType.DMA((number,)),
        ],
        out_shape=[packed] * number,
        compiler_params=pltpu.CompilerParams(vmem_limit_bytes=5 << 20),
        cost_estimate=pl.CostEstimate(flops=0, bytes_accessed=5 << 20, transcendentals=0),
        name="pack",
    )(*first, *second, *notes)


def add_tiles(which, blocks_dev, plan_ref, tile_ref, pool, total):
    tile_total = tile_ref.shape[0]
    sources = pool.shape[0] - 1
    entries = pairs_of(tile_total, blocks_dev)
    slot_bits = log(tile_total)
    pos_bits = log(sources) + 1

    def turn(step, carry):
        products = []
        for lane in range(unroll):
            code = plan_ref[which * entries + step * unroll + lane]
            left, right = [], []
            for _ in range(2):
                left.append(tile_ref[code & (tile_total - 1)].astype(jnp.bfloat16))
                code = lax.shift_right_logical(code, slot_bits)
                right.append(pool[code & ((1 << pos_bits) - 1)])
                code = lax.shift_right_logical(code, pos_bits)
            product = jnp.dot(
                jnp.concatenate(left, axis=1),
                jnp.concatenate(right, axis=0),
                preferred_element_type=jnp.float32,
            )
            products.append((code, product))
        for target, product in products:
            total[target] += product
        return carry

    count = plan_ref[2 * kinds * entries + which]
    lax.fori_loop(0, (count + unroll - 1) // unroll, turn, 0)


def put(pool, along_z, along_y, away):
    half = pool.shape[1] // 2
    top, low = slice(0, half), slice(half, 2 * half)
    for d in range(side):
        for j in range(picks):
            spot = spot_of(d, j, half)
            pool[(back(away) * side + d) * picks + j, top, :] = along_z[spot, :].astype(pool.dtype)
            pool[(d * side + back(away)) * picks + j, low, :] = along_y[spot, :].astype(pool.dtype)


def fill(need_ref, *refs):
    first, second = refs[:side], refs[side : 2 * side]
    early, pool = refs[2 * side : -1], refs[-1]
    half = pool.shape[1] // 2
    top, low = slice(0, half), slice(half, 2 * half)
    my_z = lax.axis_index("row") // side
    my_y = lax.axis_index("row") % side
    for d in range(side):
        next_y = lax.rem(my_y + d, side)
        next_z = lax.rem(my_z + d, side)
        for j in range(picks):
            mine = need_ref[j, my_z * side + next_y]
            pool[d * picks + j, top, :] = first[d][half_at(mine, half), :].astype(pool.dtype)
            mine = need_ref[j, next_z * side + my_y]
            pool[d * side * picks + j, low, :] = second[d][half_at(mine, half), :].astype(
                pool.dtype
            )
    for at, away in enumerate(near):
        put(pool, early[2 * at], early[2 * at + 1], away)
    pool[side * side * picks] = jnp.zeros(pool.shape[1:], pool.dtype)


def fill_early(need, first, second, along_z, along_y, edge):
    early = [v for away in near for v in (along_z[away - 1], along_y[away - 1])]
    return pl.pallas_call(
        fill,
        in_specs=[in_smem] + [in_vmem] * (2 * side + len(early)),
        out_specs=in_vmem,
        out_shape=jax.ShapeDtypeStruct((side * side * picks + 1, edge, span), jnp.bfloat16),
        compiler_params=pltpu.CompilerParams(vmem_limit_bytes=8 << 20),
        cost_estimate=pl.CostEstimate(flops=0, bytes_accessed=5 << 20, transcendentals=0),
        name="fill",
    )(need, *first, *second, *early)


def combine(blocks_dev, plan_ref, tile_ref, along_z, along_y, _, total, pool, listed, sem):
    copy = pltpu.make_async_copy(plan_ref, listed, sem)
    copy.start()
    total[...] = jnp.zeros_like(total)
    put(pool, along_z, along_y, side // 2)
    copy.wait()
    add_tiles(0, blocks_dev, listed, tile_ref, pool, total)


def combine_sent(listed, tiles, along_z, along_y, pool, blocks_dev):
    edge = tiles.shape[1]
    far = side // 2 - 1
    return pl.pallas_call(
        lambda *refs: combine(blocks_dev, *refs),
        in_specs=[in_vmem] * 5,
        out_specs=[in_vmem] * 2,
        scratch_shapes=[pltpu.SMEM(listed.shape, jnp.int32), pltpu.SemaphoreType.DMA(())],
        out_shape=[
            jax.ShapeDtypeStruct((places_of(0, blocks_dev), edge, span), jnp.float32),
            jax.ShapeDtypeStruct(pool.shape, pool.dtype),
        ],
        input_output_aliases={4: 1},
        compiler_params=pltpu.CompilerParams(vmem_limit_bytes=10 << 20),
        cost_estimate=pl.CostEstimate(flops=2 << 30, bytes_accessed=6 << 20, transcendentals=0),
        name="combine",
    )(listed, tiles, along_z[far], along_y[far], pool)


def combine_listed(which_ones, listed, tiles, pool, blocks_dev):
    edge = tiles.shape[1]

    def body(plan_ref, tile_ref, pool_ref, *refs):
        totals, (lists, sem) = refs[:-2], refs[-2:]
        copy = pltpu.make_async_copy(plan_ref, lists, sem)
        copy.start()
        for total in totals:
            total[...] = jnp.zeros_like(total)
        copy.wait()
        for which, total in zip(which_ones, totals):
            add_tiles(which, blocks_dev, lists, tile_ref, pool_ref, total)

    return pl.pallas_call(
        body,
        in_specs=[in_vmem] * 3,
        out_specs=[in_vmem] * len(which_ones),
        scratch_shapes=[pltpu.SMEM(listed.shape, jnp.int32), pltpu.SemaphoreType.DMA(())],
        out_shape=[
            jax.ShapeDtypeStruct((places_of(which, blocks_dev), edge, span), jnp.float32)
            for which in which_ones
        ],
        compiler_params=pltpu.CompilerParams(vmem_limit_bytes=6 << 20),
        cost_estimate=pl.CostEstimate(flops=2 << 30, bytes_accessed=8 << 20, transcendentals=0),
        name="listed",
    )(listed, tiles, pool)


def mix(group, feature_ref, keep, arrived, from_right, from_left, left_held, right_held, piece):
    part = slice(group * span, (group + 1) * span)
    pieces = keep.shape[0] // lanes // 2
    shift = 0 if left_held.shape[0] > lanes else piece
    whole = slice(piece * lanes, (piece + 1) * lanes)
    own = slice((piece - shift) * lanes, (piece - shift + 1) * lanes)
    mixed = []
    for low, ready, held in ((0, from_right, left_held), (1, from_left, right_held)):
        spot = slice((low * pieces + piece) * lanes, (low * pieces + piece + 1) * lanes)
        summed = keep[spot, :] + arrived[spot, :] + ready[whole, :] + held[own, :]
        mixed.append(((1.0 + gin_epsilon) * feature_ref[spot, part] + summed).astype(jnp.bfloat16))
    return mixed


def begin_mlp(feature_ref, w_ref, bias_ref, *refs):
    totals, (out_ref, mixed) = refs[:-2], refs[-2:]
    for piece in range(mixed.shape[0] // lanes // 2):
        for low, value in enumerate(mix(0, feature_ref, *totals, piece)):
            mixed[(2 * piece + low) * lanes : (2 * piece + low + 1) * lanes, :] = value

    def turn(step, carry):
        part = pl.ds(pl.multiple_of(step * chunk, chunk), chunk)
        out_ref[part, :] = (
            jnp.dot(mixed[part, :], w_ref[:span, :], preferred_element_type=jnp.float32)
            + bias_ref[...]
        )
        return carry

    lax.fori_loop(0, out_ref.shape[0] // chunk, turn, 0)


def end_mlp(piece, feature_ref, w_ref, before_ref, w_out_ref, bias_ref, *refs):
    totals = refs[:6]
    if piece == 0:
        result, mixed = refs[6:]
    else:
        before_result, out_ref, mixed, result, sems = refs[6:]

        def move(source, at, low):
            start = (low * out_ref.shape[0] // 2) + at * lanes
            return pltpu.make_async_copy(
                source.at[low * lanes : (low + 1) * lanes, :],
                out_ref.at[start : start + lanes, :],
                sems.at[2 * at + low],
            )

        copies = [move(before_result, 0, low) for low in range(2)]
        for copy in copies:
            copy.start()
    for low, value in enumerate(mix(1, feature_ref, *totals, piece)):
        mixed[low * lanes : (low + 1) * lanes, :] = value
    rows = mixed.shape[0]
    hidden = before_ref[piece * rows : (piece + 1) * rows, :] + jnp.dot(
        mixed[...], w_ref[span:, :], preferred_element_type=jnp.float32
    )
    hidden = jnp.maximum(hidden, 0.0).astype(jnp.bfloat16)
    updated = jnp.dot(hidden, w_out_ref[...], preferred_element_type=jnp.float32)
    result[...] = (updated + bias_ref[...]).astype(result.dtype)
    if piece == 0:
        return
    for low in range(2):
        copies.append(move(result, piece, low))
        copies[-1].start()
    for copy in copies:
        copy.wait()


def on_device(
    features, tiles, tile_rows, tile_cols, tile_count, needed, w_in, bias_in, w_out, bias_out
):
    edge = tiles.shape[-1]
    half = edge // 2
    nodes, width = features.shape
    blocks_dev = nodes // edge
    hidden_size = w_in.shape[1]
    blocks = places_of(1, blocks_dev)
    groups = width // span

    need = needed[0, 0].T
    firsts, seconds = [], []
    for group in range(groups):
        top, low = split_group(group, features, need)
        first = [top] + [None] * (side - 1)
        second = [low] + [None] * (side - 1)
        for away in (1, 3, 2):
            first[away] = from_y(first[0], away)
            second[away] = from_z(second[0], away)
        firsts.append(first)
        seconds.append(second)
    notes = seconds[0][1:] + firsts[0][1:]

    listed = pl.pallas_call(
        lambda *refs: plan(*refs, blocks_dev),
        in_specs=[in_smem] * 3,
        out_specs=in_smem,
        out_shape=jax.ShapeDtypeStruct((512,), jnp.int32),
        scratch_shapes=[pltpu.SMEM((2 * kinds * (blocks + 1),), jnp.int32)],
        compiler_params=pltpu.CompilerParams(vmem_limit_bytes=1 << 20),
        cost_estimate=pl.CostEstimate(flops=0, bytes_accessed=1 << 20, transcendentals=0),
        name="plan",
    )(tile_rows[0, 0], tile_cols[0, 0], tile_count)
    cell_tiles = tiles[0, 0]

    sums = []
    for group in range(groups):
        first, second = firsts[group], seconds[group]
        packed = pack_group(first, second, notes, half)
        along_z, along_y = [None] * (side - 1), [None] * (side - 1)
        for away in (1, 3, 2):
            along_z[away - 1] = from_z(packed[away - 1], -away)
            along_y[away - 1] = from_y(packed[side + away - 2], -away)
        pool = fill_early(need, first, second, along_z, along_y, edge)
        send, pool = combine_sent(listed, cell_tiles, along_z, along_y, pool, blocks_dev)
        arrived = lax.ppermute(send, "col", col_shift(0, 1))
        keep, sides = combine_listed((kinds, 1), listed, cell_tiles, pool, blocks_dev)
        over_right, over_left = pl.pallas_call(
            join_across,
            in_specs=[in_vmem] * 2,
            out_specs=[in_vmem] * 2,
            out_shape=[jax.ShapeDtypeStruct((blocks_dev // 2, edge, span), jnp.float32)] * 2,
            compiler_params=pltpu.CompilerParams(vmem_limit_bytes=4 << 20),
            cost_estimate=pl.CostEstimate(flops=0, bytes_accessed=2 << 20, transcendentals=0),
            name="join",
        )(keep, arrived)
        relay_right = lax.ppermute(over_right, "col", col_shift(1, 0))
        relay_left = lax.ppermute(over_left, "col", col_shift(-1, 0))
        arrived = lax.ppermute(sides, "col", col_shift(0, 1))
        keep, mine_sent, mine_kept = combine_listed(
            (kinds + 1, 2, kinds + 2), listed, cell_tiles, pool, blocks_dev
        )
        cut = blocks_dev // 2
        held = [cut] if group < groups - 1 else [1] * cut
        sizes = held + [cut, cut] + held
        joined = pl.pallas_call(
            join_rest,
            in_specs=[in_vmem] * 2,
            out_specs=[in_vmem] * len(sizes),
            out_shape=[jax.ShapeDtypeStruct((n, edge, span), jnp.float32) for n in sizes],
            compiler_params=pltpu.CompilerParams(vmem_limit_bytes=6 << 20),
            cost_estimate=pl.CostEstimate(flops=0, bytes_accessed=4 << 20, transcendentals=0),
            name="join",
        )(keep, arrived)
        right_held, (right, left) = joined[: len(held)], joined[len(held) : len(held) + 2]
        left_held = joined[len(held) + 2 :]
        from_left = lax.ppermute(right, "col", col_shift(1, 0))
        from_right = lax.ppermute(left, "col", col_shift(-1, 0))
        relayed = pl.pallas_call(
            relay,
            in_specs=[in_vmem] * (2 + 2 * len(held)),
            out_specs=[in_vmem] * (2 * len(held)),
            out_shape=[jax.ShapeDtypeStruct((n, edge, span), jnp.float32) for n in held * 2],
            compiler_params=pltpu.CompilerParams(vmem_limit_bytes=4 << 20),
            cost_estimate=pl.CostEstimate(flops=0, bytes_accessed=2 << 20, transcendentals=0),
            name="relay",
        )(relay_right, relay_left, *right_held, *left_held)
        from_left_held, from_right_held = [], []
        for piece in range(len(held)):
            from_left_held.append(
                lax.ppermute(relayed[piece], "col", col_shift(1, 0))
            )
            from_right_held.append(
                lax.ppermute(relayed[len(held) + piece], "col", col_shift(-1, 0))
            )
        arrived = lax.ppermute(mine_sent, "col", col_shift(0, 1))
        sums.append((mine_kept, arrived, from_right, from_left, from_left_held, from_right_held))

    flat = [[jax.tree.map(lambda v: v.reshape(-1, span), part) for part in one] for one in sums]
    *ready, (left_part,), (right_part,) = flat[0]
    before = pl.pallas_call(
        begin_mlp,
        in_specs=[in_vmem] * 9,
        out_specs=in_vmem,
        out_shape=jax.ShapeDtypeStruct((nodes, hidden_size), jnp.float32),
        scratch_shapes=[pltpu.VMEM((nodes, span), jnp.bfloat16)],
        compiler_params=pltpu.CompilerParams(vmem_limit_bytes=8 << 20),
        cost_estimate=pl.CostEstimate(
            flops=1 << 29, bytes_accessed=8 << 20, transcendentals=0
        ),
        name="begin",
    )(features, w_in, bias_in.reshape(1, -1), *ready, left_part, right_part)
    updated = []
    *ready, left_parts, right_parts = flat[1]
    for piece in range(len(left_parts)):
        rows = nodes // len(left_parts)
        last = piece == len(left_parts) - 1
        updated = [
            pl.pallas_call(
                lambda *refs: end_mlp(piece, *refs),
                in_specs=[in_vmem] * (11 + len(updated)),
                out_specs=pl.BlockSpec(memory_space=pltpu.HBM) if last else in_vmem,
                out_shape=jax.ShapeDtypeStruct((nodes if last else rows, width), jnp.bfloat16),
                scratch_shapes=[pltpu.VMEM((rows, span), jnp.bfloat16)]
                + (
                    [pltpu.VMEM((rows, width), jnp.bfloat16), pltpu.SemaphoreType.DMA((4,))]
                    if last
                    else []
                ),
                compiler_params=pltpu.CompilerParams(vmem_limit_bytes=8 << 20),
                cost_estimate=pl.CostEstimate(
                    flops=3 << 28, bytes_accessed=4 << 20, transcendentals=0
                ),
                name="end",
            )(
                features,
                w_in,
                before,
                w_out,
                bias_out.reshape(1, -1),
                *ready,
                left_parts[piece],
                right_parts[piece],
                *updated,
            )
        ]
    return updated[0]


def solution(mesh):
    placed = (
        P(("row", "col"), None),
        P("row", "col", None, None, None),
        P("row", "col", None),
        P("row", "col", None),
        P("row", "col"),
        P("row", "col", None, None),
        P(),
        P(),
        P(),
        P(),
    )

    return jax.shard_map(
        on_device, mesh=mesh, in_specs=placed, out_specs=P(("row", "col"), None), check_vma=False
    )
```

```python
import jax
import jax.numpy as jnp
from jax import lax
from jax.experimental import pallas as pl
from jax.experimental.pallas import tpu as pltpu
from jax.sharding import PartitionSpec as P


gin_epsilon = 0.25
unroll = 8
span = 256
side = 4
cores = 2
picks = 2
kinds = 3
across_x = side // 2
near = (1, 3)
note_rows = 8
lanes = 128
chunk = 256

in_vmem = pl.BlockSpec(memory_space=pltpu.VMEM)
in_smem = pl.BlockSpec(memory_space=pltpu.SMEM)


def row_shift(step_z, step_y):
    return [
        (z * side + y, (z + step_z) % side * side + (y + step_y) % side)
        for z in range(side)
        for y in range(side)
    ]


def col_shift(step_x, step_core):
    return [
        (x * cores + k, (x + step_x) % side * cores + (k + step_core) % cores)
        for x in range(side)
        for k in range(cores)
    ]


def from_z(value, step):
    return lax.ppermute(value, "row", row_shift(-step, 0))


def from_y(value, step):
    return lax.ppermute(value, "row", row_shift(0, -step))


def back(step):
    return (side - step) % side


def half_at(number, half):
    return pl.ds(pl.multiple_of(number * half, half), half)


def spot_of(d, j, half):
    return slice((d * picks + j) * half, (d * picks + j + 1) * half)


def split(group, feature_ref, *refs):
    noted = group == 0
    if noted:
        need_ref, first_ref, second_ref, need, sems = refs
    else:
        first_ref, second_ref, sems = refs
    half = lanes // 2
    rows = feature_ref.shape[0] // 2
    part = slice(group * span, (group + 1) * span)
    copies = []
    for place, out in enumerate((first_ref, second_ref)):
        for block in range(rows // half):
            start = (2 * block + place) * half
            copies.append(
                pltpu.make_async_copy(
                    feature_ref.at[start : start + half, part],
                    out.at[block * half : (block + 1) * half, :],
                    sems.at[len(copies)],
                )
            )
    if noted:
        copy = pltpu.make_async_copy(need_ref, need, sems.at[len(copies)])
        copy.start()
    for each in copies:
        each.start()
    if noted:
        copy.wait()
        note = need[...].astype(jnp.float32)
        for out in (first_ref, second_ref):
            out[rows:, :] = jnp.zeros((note_rows, span), jnp.float32)
            out[rows : rows + note.shape[0], : note.shape[1]] = note
    for each in copies:
        each.wait()


def split_group(group, features, need):
    nodes = features.shape[0]
    args = [features] + ([need] if group == 0 else [])
    rows = nodes // 2 + (note_rows if group == 0 else 0)
    copies = nodes // lanes * 2 + (1 if group == 0 else 0)
    return pl.pallas_call(
        lambda *refs: split(group, *refs),
        in_specs=[pl.BlockSpec(memory_space=pltpu.HBM)] * len(args),
        out_specs=[in_vmem] * 2,
        scratch_shapes=([pltpu.VMEM(need.shape, jnp.int32)] if group == 0 else [])
        + [pltpu.SemaphoreType.DMA((copies,))],
        out_shape=[jax.ShapeDtypeStruct((rows, span), jnp.float32)] * 2,
        compiler_params=pltpu.CompilerParams(vmem_limit_bytes=4 << 20),
        cost_estimate=pl.CostEstimate(flops=0, bytes_accessed=1 << 20, transcendentals=0),
        name="split",
    )(*[pltpu.with_memory_space_constraint(v, pltpu.HBM) for v in args])


def join_across(keep_ref, arrived_ref, over_right_ref, over_left_ref):
    cut = over_right_ref.shape[0]
    over_right_ref[...] = keep_ref[:cut] + arrived_ref[:cut]
    over_left_ref[...] = keep_ref[cut:] + arrived_ref[cut:]


def join_rest(keep_ref, arrived_ref, *outs):
    start = 0
    for out in outs:
        spot = slice(start, start + out.shape[0])
        out[...] = keep_ref[spot] + arrived_ref[spot]
        start = spot.stop


def relay(from_left_ref, from_right_ref, *refs):
    helds, outs = refs[: len(refs) // 2], refs[len(refs) // 2 :]
    pieces = len(outs) // 2
    for at, (held, out) in enumerate(zip(helds, outs)):
        size = out.shape[0]
        source = from_left_ref if at < pieces else from_right_ref
        start = at % pieces * size
        out[...] = held[...] + source[start : start + size]


def log(value):
    return value.bit_length() - 1


def places_of(which, blocks_dev):
    return blocks_dev * (2 if which % kinds == 1 else 1)


def pairs_of(tile_total, blocks_dev):
    return (tile_total + places_of(1, blocks_dev)) // 2 + unroll


def plan(row_ref, col_ref, count_ref, plan_ref, waiting, blocks_dev):
    tile_total = row_ref.shape[0]
    blocks = places_of(1, blocks_dev)
    entries = pairs_of(tile_total, blocks_dev)
    slot_bits = log(tile_total)
    code_bits = slot_bits + log(side * side * picks) + 1
    empty = (side * side * picks) << slot_bits
    my_z = lax.axis_index("row") // side
    my_y = lax.axis_index("row") % side
    my_x = lax.axis_index("col") // cores
    my_core = lax.axis_index("col") % cores

    def pair(place, first, second):
        return first | (second << code_bits) | (place << (2 * code_bits))

    for place in range(2 * kinds * blocks):
        waiting[place] = -1
    for which in range(2 * kinds):
        waiting[2 * kinds * blocks + which] = 0

    def turn(slot, carry):
        target = row_ref[slot]
        source = col_ref[slot]
        column = lax.shift_right_logical(target, log(blocks_dev))
        away_x = (lax.shift_right_logical(column, log(cores)) - my_x) & (side - 1)
        beside = away_x & 1
        kind = jnp.where(beside == 1, 1, jnp.where(away_x == across_x, 0, 2))
        right = (away_x > across_x).astype(jnp.int32)
        place = right * blocks_dev + (target & (blocks_dev - 1))
        which = kinds * (1 - ((column & (cores - 1)) ^ my_core)) + kind
        owner = lax.shift_right_logical(source, log(picks))
        away_z = (lax.shift_right_logical(owner, log(side)) - my_z) & (side - 1)
        away_y = (owner - my_y) & (side - 1)
        pos = (away_z * side + away_y) * picks + (source & (picks - 1))
        code = slot | (pos << slot_bits)
        before = waiting[which * blocks + place]
        end = waiting[2 * kinds * blocks + which]
        plan_ref[which * entries + end] = pair(place, before, code)
        waiting[which * blocks + place] = jnp.where(before >= 0, -1, code)
        waiting[2 * kinds * blocks + which] = end + (before >= 0).astype(jnp.int32)
        return carry

    lax.fori_loop(0, count_ref[0, 0], turn, 0)
    for which in range(2 * kinds):
        end = waiting[2 * kinds * blocks + which]
        for place in range(places_of(which, blocks_dev)):
            before = waiting[which * blocks + place]
            plan_ref[which * entries + end] = pair(place, before, empty)
            end = end + (before >= 0).astype(jnp.int32)
        for extra in range(unroll):
            plan_ref[which * entries + end + extra] = pair(0, empty, empty)
        plan_ref[2 * kinds * entries + which] = end


def pack(half, *refs):
    first, second = refs[:side], refs[side : 2 * side]
    notes_from = refs[2 * side : 4 * side - 2]
    outs = refs[4 * side - 2 : 6 * side - 4]
    notes, sems = refs[6 * side - 4 :]
    rows = side * half
    copies = [
        pltpu.make_async_copy(
            source.at[rows : rows + note_rows, :lanes], notes.at[at], sems.at[at]
        )
        for at, source in enumerate(notes_from)
    ]
    for copy in copies:
        copy.start()
    for copy in copies:
        copy.wait()
    my_z = lax.axis_index("row") // side
    my_y = lax.axis_index("row") % side
    for away in range(1, side):
        for d in range(side):
            next_y = lax.rem(my_y + d, side)
            next_z = lax.rem(my_z + d, side)
            for j in range(picks):
                spot = spot_of(d, j, half)
                along_z = notes[away - 1, j, my_z * side + next_y].astype(jnp.int32)
                outs[away - 1][spot, :] = first[d][half_at(along_z, half), :]
                along_y = notes[side + away - 2, j, next_z * side + my_y].astype(jnp.int32)
                outs[side + away - 2][spot, :] = second[d][half_at(along_y, half), :]


def pack_group(first, second, notes, half):
    packed = jax.ShapeDtypeStruct((side * picks * half, span), jnp.float32)
    number = 2 * (side - 1)
    return pl.pallas_call(
        lambda *refs: pack(half, *refs),
        in_specs=[in_vmem] * (2 * side + number),
        out_specs=[in_vmem] * number,
        scratch_shapes=[
            pltpu.SMEM((number, note_rows, lanes), jnp.float32),
            pltpu.SemaphoreType.DMA((number,)),
        ],
        out_shape=[packed] * number,
        compiler_params=pltpu.CompilerParams(vmem_limit_bytes=5 << 20),
        cost_estimate=pl.CostEstimate(flops=0, bytes_accessed=5 << 20, transcendentals=0),
        name="pack",
    )(*first, *second, *notes)


def add_tiles(which, blocks_dev, plan_ref, tile_ref, pool, total):
    tile_total = tile_ref.shape[0]
    sources = pool.shape[0] - 1
    entries = pairs_of(tile_total, blocks_dev)
    slot_bits = log(tile_total)
    pos_bits = log(sources) + 1

    def turn(step, carry):
        products = []
        for lane in range(unroll):
            code = plan_ref[which * entries + step * unroll + lane]
            left, right = [], []
            for _ in range(2):
                left.append(tile_ref[code & (tile_total - 1)].astype(jnp.bfloat16))
                code = lax.shift_right_logical(code, slot_bits)
                right.append(pool[code & ((1 << pos_bits) - 1)])
                code = lax.shift_right_logical(code, pos_bits)
            product = jnp.dot(
                jnp.concatenate(left, axis=1),
                jnp.concatenate(right, axis=0),
                preferred_element_type=jnp.float32,
            )
            products.append((code, product))
        for target, product in products:
            total[target] += product
        return carry

    count = plan_ref[2 * kinds * entries + which]
    lax.fori_loop(0, (count + unroll - 1) // unroll, turn, 0)


def put(pool, along_z, along_y, away):
    half = pool.shape[1] // 2
    top, low = slice(0, half), slice(half, 2 * half)
    for d in range(side):
        for j in range(picks):
            spot = spot_of(d, j, half)
            pool[(back(away) * side + d) * picks + j, top, :] = along_z[spot, :].astype(pool.dtype)
            pool[(d * side + back(away)) * picks + j, low, :] = along_y[spot, :].astype(pool.dtype)


def fill(need_ref, *refs):
    first, second = refs[:side], refs[side : 2 * side]
    early, pool = refs[2 * side : -1], refs[-1]
    half = pool.shape[1] // 2
    top, low = slice(0, half), slice(half, 2 * half)
    my_z = lax.axis_index("row") // side
    my_y = lax.axis_index("row") % side
    for d in range(side):
        next_y = lax.rem(my_y + d, side)
        next_z = lax.rem(my_z + d, side)
        for j in range(picks):
            mine = need_ref[j, my_z * side + next_y]
            pool[d * picks + j, top, :] = first[d][half_at(mine, half), :].astype(pool.dtype)
            mine = need_ref[j, next_z * side + my_y]
            pool[d * side * picks + j, low, :] = second[d][half_at(mine, half), :].astype(
                pool.dtype
            )
    for at, away in enumerate(near):
        put(pool, early[2 * at], early[2 * at + 1], away)
    pool[side * side * picks] = jnp.zeros(pool.shape[1:], pool.dtype)


def fill_early(need, first, second, along_z, along_y, edge):
    early = [v for away in near for v in (along_z[away - 1], along_y[away - 1])]
    return pl.pallas_call(
        fill,
        in_specs=[in_smem] + [in_vmem] * (2 * side + len(early)),
        out_specs=in_vmem,
        out_shape=jax.ShapeDtypeStruct((side * side * picks + 1, edge, span), jnp.bfloat16),
        compiler_params=pltpu.CompilerParams(vmem_limit_bytes=8 << 20),
        cost_estimate=pl.CostEstimate(flops=0, bytes_accessed=5 << 20, transcendentals=0),
        name="fill",
    )(need, *first, *second, *early)


def combine(blocks_dev, plan_ref, tile_ref, along_z, along_y, _, total, pool, listed, sem):
    copy = pltpu.make_async_copy(plan_ref, listed, sem)
    copy.start()
    total[...] = jnp.zeros_like(total)
    put(pool, along_z, along_y, side // 2)
    copy.wait()
    add_tiles(0, blocks_dev, listed, tile_ref, pool, total)


def combine_sent(listed, tiles, along_z, along_y, pool, blocks_dev):
    edge = tiles.shape[1]
    far = side // 2 - 1
    return pl.pallas_call(
        lambda *refs: combine(blocks_dev, *refs),
        in_specs=[in_vmem] * 5,
        out_specs=[in_vmem] * 2,
        scratch_shapes=[pltpu.SMEM(listed.shape, jnp.int32), pltpu.SemaphoreType.DMA(())],
        out_shape=[
            jax.ShapeDtypeStruct((places_of(0, blocks_dev), edge, span), jnp.float32),
            jax.ShapeDtypeStruct(pool.shape, pool.dtype),
        ],
        input_output_aliases={4: 1},
        compiler_params=pltpu.CompilerParams(vmem_limit_bytes=10 << 20),
        cost_estimate=pl.CostEstimate(flops=2 << 30, bytes_accessed=6 << 20, transcendentals=0),
        name="combine",
    )(listed, tiles, along_z[far], along_y[far], pool)


def combine_listed(which_ones, listed, tiles, pool, blocks_dev):
    edge = tiles.shape[1]

    def body(plan_ref, tile_ref, pool_ref, *refs):
        totals, (lists, sem) = refs[:-2], refs[-2:]
        copy = pltpu.make_async_copy(plan_ref, lists, sem)
        copy.start()
        for total in totals:
            total[...] = jnp.zeros_like(total)
        copy.wait()
        for which, total in zip(which_ones, totals):
            add_tiles(which, blocks_dev, lists, tile_ref, pool_ref, total)

    return pl.pallas_call(
        body,
        in_specs=[in_vmem] * 3,
        out_specs=[in_vmem] * len(which_ones),
        scratch_shapes=[pltpu.SMEM(listed.shape, jnp.int32), pltpu.SemaphoreType.DMA(())],
        out_shape=[
            jax.ShapeDtypeStruct((places_of(which, blocks_dev), edge, span), jnp.float32)
            for which in which_ones
        ],
        compiler_params=pltpu.CompilerParams(vmem_limit_bytes=6 << 20),
        cost_estimate=pl.CostEstimate(flops=2 << 30, bytes_accessed=8 << 20, transcendentals=0),
        name="listed",
    )(listed, tiles, pool)


def mix(group, feature_ref, keep, arrived, from_right, from_left, left_held, right_held, piece):
    part = slice(group * span, (group + 1) * span)
    pieces = keep.shape[0] // lanes // 2
    shift = 0 if left_held.shape[0] > lanes else piece
    whole = slice(piece * lanes, (piece + 1) * lanes)
    own = slice((piece - shift) * lanes, (piece - shift + 1) * lanes)
    mixed = []
    for low, ready, held in ((0, from_right, left_held), (1, from_left, right_held)):
        spot = slice((low * pieces + piece) * lanes, (low * pieces + piece + 1) * lanes)
        summed = keep[spot, :] + arrived[spot, :] + ready[whole, :] + held[own, :]
        mixed.append(((1.0 + gin_epsilon) * feature_ref[spot, part] + summed).astype(jnp.bfloat16))
    return mixed


def begin_mlp(feature_ref, w_ref, bias_ref, *refs):
    totals, (out_ref, mixed) = refs[:-2], refs[-2:]
    for piece in range(mixed.shape[0] // lanes // 2):
        for low, value in enumerate(mix(0, feature_ref, *totals, piece)):
            mixed[(2 * piece + low) * lanes : (2 * piece + low + 1) * lanes, :] = value

    def turn(step, carry):
        part = pl.ds(pl.multiple_of(step * chunk, chunk), chunk)
        out_ref[part, :] = (
            jnp.dot(mixed[part, :], w_ref[:span, :], preferred_element_type=jnp.float32)
            + bias_ref[...]
        )
        return carry

    lax.fori_loop(0, out_ref.shape[0] // chunk, turn, 0)


def end_mlp(piece, feature_ref, w_ref, before_ref, w_out_ref, bias_ref, *refs):
    totals = refs[:6]
    if piece == 0:
        result, mixed = refs[6:]
    else:
        before_result, out_ref, mixed, result, sems = refs[6:]

        def move(source, at, low, columns):
            start = (low * out_ref.shape[0] // 2) + at * lanes
            copies.append(
                pltpu.make_async_copy(
                    source.at[low * lanes : (low + 1) * lanes, columns],
                    out_ref.at[start : start + lanes, columns],
                    sems.at[len(copies)],
                )
            )
            return copies[-1]

        copies = []
        for low in range(2):
            move(before_result, 0, low, slice(None))
        for copy in copies:
            copy.start()
    for low, value in enumerate(mix(1, feature_ref, *totals, piece)):
        mixed[low * lanes : (low + 1) * lanes, :] = value
    rows = mixed.shape[0]
    hidden = before_ref[piece * rows : (piece + 1) * rows, :] + jnp.dot(
        mixed[...], w_ref[span:, :], preferred_element_type=jnp.float32
    )
    hidden = jnp.maximum(hidden, 0.0).astype(jnp.bfloat16)
    for start in range(0, result.shape[1], span):
        columns = slice(start, start + span)
        updated = jnp.dot(hidden, w_out_ref[:, columns], preferred_element_type=jnp.float32)
        result[:, columns] = (updated + bias_ref[:, columns]).astype(result.dtype)
        for low in range(2 if piece else 0):
            move(result, 1, low, columns).start()
    for copy in copies if piece else []:
        copy.wait()


def on_device(
    features, tiles, tile_rows, tile_cols, tile_count, needed, w_in, bias_in, w_out, bias_out
):
    edge = tiles.shape[-1]
    half = edge // 2
    nodes, width = features.shape
    blocks_dev = nodes // edge
    hidden_size = w_in.shape[1]
    blocks = places_of(1, blocks_dev)
    groups = width // span

    need = needed[0, 0].T
    firsts, seconds = [], []
    for group in range(groups):
        top, low = split_group(group, features, need)
        first = [top] + [None] * (side - 1)
        second = [low] + [None] * (side - 1)
        for away in (1, 3, 2):
            first[away] = from_y(first[0], away)
            second[away] = from_z(second[0], away)
        firsts.append(first)
        seconds.append(second)
    notes = seconds[0][1:] + firsts[0][1:]

    listed = pl.pallas_call(
        lambda *refs: plan(*refs, blocks_dev),
        in_specs=[in_smem] * 3,
        out_specs=in_smem,
        out_shape=jax.ShapeDtypeStruct((512,), jnp.int32),
        scratch_shapes=[pltpu.SMEM((2 * kinds * (blocks + 1),), jnp.int32)],
        compiler_params=pltpu.CompilerParams(vmem_limit_bytes=1 << 20),
        cost_estimate=pl.CostEstimate(flops=0, bytes_accessed=1 << 20, transcendentals=0),
        name="plan",
    )(tile_rows[0, 0], tile_cols[0, 0], tile_count)
    cell_tiles = tiles[0, 0]

    sums = []
    for group in range(groups):
        first, second = firsts[group], seconds[group]
        packed = pack_group(first, second, notes, half)
        along_z, along_y = [None] * (side - 1), [None] * (side - 1)
        for away in (1, 3, 2):
            along_z[away - 1] = from_z(packed[away - 1], -away)
            along_y[away - 1] = from_y(packed[side + away - 2], -away)
        pool = fill_early(need, first, second, along_z, along_y, edge)
        send, pool = combine_sent(listed, cell_tiles, along_z, along_y, pool, blocks_dev)
        arrived = lax.ppermute(send, "col", col_shift(0, 1))
        keep, sides = combine_listed((kinds, 1), listed, cell_tiles, pool, blocks_dev)
        over_right, over_left = pl.pallas_call(
            join_across,
            in_specs=[in_vmem] * 2,
            out_specs=[in_vmem] * 2,
            out_shape=[jax.ShapeDtypeStruct((blocks_dev // 2, edge, span), jnp.float32)] * 2,
            compiler_params=pltpu.CompilerParams(vmem_limit_bytes=4 << 20),
            cost_estimate=pl.CostEstimate(flops=0, bytes_accessed=2 << 20, transcendentals=0),
            name="join",
        )(keep, arrived)
        relay_right = lax.ppermute(over_right, "col", col_shift(1, 0))
        relay_left = lax.ppermute(over_left, "col", col_shift(-1, 0))
        arrived = lax.ppermute(sides, "col", col_shift(0, 1))
        keep, mine_sent, mine_kept = combine_listed(
            (kinds + 1, 2, kinds + 2), listed, cell_tiles, pool, blocks_dev
        )
        cut = blocks_dev // 2
        held = [cut] if group < groups - 1 else [1] * cut
        sizes = held + [cut, cut] + held
        joined = pl.pallas_call(
            join_rest,
            in_specs=[in_vmem] * 2,
            out_specs=[in_vmem] * len(sizes),
            out_shape=[jax.ShapeDtypeStruct((n, edge, span), jnp.float32) for n in sizes],
            compiler_params=pltpu.CompilerParams(vmem_limit_bytes=6 << 20),
            cost_estimate=pl.CostEstimate(flops=0, bytes_accessed=4 << 20, transcendentals=0),
            name="join",
        )(keep, arrived)
        right_held, (right, left) = joined[: len(held)], joined[len(held) : len(held) + 2]
        left_held = joined[len(held) + 2 :]
        from_left = lax.ppermute(right, "col", col_shift(1, 0))
        from_right = lax.ppermute(left, "col", col_shift(-1, 0))
        relayed = pl.pallas_call(
            relay,
            in_specs=[in_vmem] * (2 + 2 * len(held)),
            out_specs=[in_vmem] * (2 * len(held)),
            out_shape=[jax.ShapeDtypeStruct((n, edge, span), jnp.float32) for n in held * 2],
            compiler_params=pltpu.CompilerParams(vmem_limit_bytes=4 << 20),
            cost_estimate=pl.CostEstimate(flops=0, bytes_accessed=2 << 20, transcendentals=0),
            name="relay",
        )(relay_right, relay_left, *right_held, *left_held)
        from_left_held, from_right_held = [], []
        for piece in range(len(held)):
            from_left_held.append(
                lax.ppermute(relayed[piece], "col", col_shift(1, 0))
            )
            from_right_held.append(
                lax.ppermute(relayed[len(held) + piece], "col", col_shift(-1, 0))
            )
        arrived = lax.ppermute(mine_sent, "col", col_shift(0, 1))
        sums.append((mine_kept, arrived, from_right, from_left, from_left_held, from_right_held))

    flat = [[jax.tree.map(lambda v: v.reshape(-1, span), part) for part in one] for one in sums]
    *ready, (left_part,), (right_part,) = flat[0]
    before = pl.pallas_call(
        begin_mlp,
        in_specs=[in_vmem] * 9,
        out_specs=in_vmem,
        out_shape=jax.ShapeDtypeStruct((nodes, hidden_size), jnp.float32),
        scratch_shapes=[pltpu.VMEM((nodes, span), jnp.bfloat16)],
        compiler_params=pltpu.CompilerParams(vmem_limit_bytes=8 << 20),
        cost_estimate=pl.CostEstimate(
            flops=1 << 29, bytes_accessed=8 << 20, transcendentals=0
        ),
        name="begin",
    )(features, w_in, bias_in.reshape(1, -1), *ready, left_part, right_part)
    updated = []
    *ready, left_parts, right_parts = flat[1]
    for piece in range(len(left_parts)):
        rows = nodes // len(left_parts)
        last = piece == len(left_parts) - 1
        updated = [
            pl.pallas_call(
                lambda *refs: end_mlp(piece, *refs),
                in_specs=[in_vmem] * (11 + len(updated)),
                out_specs=pl.BlockSpec(memory_space=pltpu.HBM) if last else in_vmem,
                out_shape=jax.ShapeDtypeStruct((nodes if last else rows, width), jnp.bfloat16),
                scratch_shapes=[pltpu.VMEM((rows, span), jnp.bfloat16)]
                + (
                    [pltpu.VMEM((rows, width), jnp.bfloat16), pltpu.SemaphoreType.DMA((6,))]
                    if last
                    else []
                ),
                compiler_params=pltpu.CompilerParams(vmem_limit_bytes=8 << 20),
                cost_estimate=pl.CostEstimate(
                    flops=3 << 28, bytes_accessed=4 << 20, transcendentals=0
                ),
                name="end",
            )(
                features,
                w_in,
                before,
                w_out,
                bias_out.reshape(1, -1),
                *ready,
                left_parts[piece],
                right_parts[piece],
                *updated,
            )
        ]
    return updated[0]


def solution(mesh):
    placed = (
        P(("row", "col"), None),
        P("row", "col", None, None, None),
        P("row", "col", None),
        P("row", "col", None),
        P("row", "col"),
        P("row", "col", None, None),
        P(),
        P(),
        P(),
        P(),
    )

    return jax.shard_map(
        on_device, mesh=mesh, in_specs=placed, out_specs=P(("row", "col"), None), check_vma=False
    )
```

```python
import jax
import jax.numpy as jnp
from jax import lax
from jax.experimental import pallas as pl
from jax.experimental.pallas import tpu as pltpu
from jax.sharding import PartitionSpec as P


gin_epsilon = 0.25
unroll = 8
span = 256
side = 4
cores = 2
picks = 2
kinds = 3
across_x = side // 2
near = (1, 3)
note_rows = 8
lanes = 128
chunk = 256

in_vmem = pl.BlockSpec(memory_space=pltpu.VMEM)
in_smem = pl.BlockSpec(memory_space=pltpu.SMEM)


def row_shift(step_z, step_y):
    return [
        (z * side + y, (z + step_z) % side * side + (y + step_y) % side)
        for z in range(side)
        for y in range(side)
    ]


def col_shift(step_x, step_core):
    return [
        (x * cores + k, (x + step_x) % side * cores + (k + step_core) % cores)
        for x in range(side)
        for k in range(cores)
    ]


def from_z(value, step):
    return lax.ppermute(value, "row", row_shift(-step, 0))


def from_y(value, step):
    return lax.ppermute(value, "row", row_shift(0, -step))


def back(step):
    return (side - step) % side


def half_at(number, half):
    return pl.ds(pl.multiple_of(number * half, half), half)


def spot_of(d, j, half):
    return slice((d * picks + j) * half, (d * picks + j + 1) * half)


def split(group, feature_ref, *refs):
    noted = group == 0
    if noted:
        need_ref, first_ref, second_ref, need, sems = refs
    else:
        first_ref, second_ref, sems = refs
    half = lanes // 2
    rows = feature_ref.shape[0] // 2
    part = slice(group * span, (group + 1) * span)
    copies = []
    for place, out in enumerate((first_ref, second_ref)):
        for block in range(rows // half):
            start = (2 * block + place) * half
            copies.append(
                pltpu.make_async_copy(
                    feature_ref.at[start : start + half, part],
                    out.at[block * half : (block + 1) * half, :],
                    sems.at[len(copies)],
                )
            )
    if noted:
        copy = pltpu.make_async_copy(need_ref, need, sems.at[len(copies)])
        copy.start()
    for each in copies:
        each.start()
    if noted:
        copy.wait()
        note = need[...].astype(jnp.float32)
        for out in (first_ref, second_ref):
            out[rows:, :] = jnp.zeros((note_rows, span), jnp.float32)
            out[rows : rows + note.shape[0], : note.shape[1]] = note
    for each in copies:
        each.wait()


def split_group(group, features, need):
    nodes = features.shape[0]
    args = [features] + ([need] if group == 0 else [])
    rows = nodes // 2 + (note_rows if group == 0 else 0)
    copies = nodes // lanes * 2 + (1 if group == 0 else 0)
    return pl.pallas_call(
        lambda *refs: split(group, *refs),
        in_specs=[pl.BlockSpec(memory_space=pltpu.HBM)] * len(args),
        out_specs=[in_vmem] * 2,
        scratch_shapes=([pltpu.VMEM(need.shape, jnp.int32)] if group == 0 else [])
        + [pltpu.SemaphoreType.DMA((copies,))],
        out_shape=[jax.ShapeDtypeStruct((rows, span), jnp.float32)] * 2,
        compiler_params=pltpu.CompilerParams(vmem_limit_bytes=4 << 20),
        cost_estimate=pl.CostEstimate(flops=0, bytes_accessed=1 << 20, transcendentals=0),
        name="split",
    )(*[pltpu.with_memory_space_constraint(v, pltpu.HBM) for v in args])


def join_across(keep_ref, arrived_ref, over_right_ref, over_left_ref):
    cut = over_right_ref.shape[0]
    over_right_ref[...] = keep_ref[:cut] + arrived_ref[:cut]
    over_left_ref[...] = keep_ref[cut:] + arrived_ref[cut:]


def join_rest(keep_ref, arrived_ref, *outs):
    start = 0
    for out in outs:
        spot = slice(start, start + out.shape[0])
        out[...] = keep_ref[spot] + arrived_ref[spot]
        start = spot.stop


def relay(from_left_ref, from_right_ref, *refs):
    helds, outs = refs[: len(refs) // 2], refs[len(refs) // 2 :]
    pieces = len(outs) // 2
    for at, (held, out) in enumerate(zip(helds, outs)):
        size = out.shape[0]
        source = from_left_ref if at < pieces else from_right_ref
        start = at % pieces * size
        out[...] = held[...] + source[start : start + size]


def log(value):
    return value.bit_length() - 1


def places_of(which, blocks_dev):
    return blocks_dev * (2 if which % kinds == 1 else 1)


def pairs_of(tile_total, blocks_dev):
    return (tile_total + places_of(1, blocks_dev)) // 2 + unroll


def plan(row_ref, col_ref, count_ref, plan_ref, waiting, blocks_dev):
    tile_total = row_ref.shape[0]
    blocks = places_of(1, blocks_dev)
    entries = pairs_of(tile_total, blocks_dev)
    slot_bits = log(tile_total)
    code_bits = slot_bits + log(side * side * picks) + 1
    empty = (side * side * picks) << slot_bits
    my_z = lax.axis_index("row") // side
    my_y = lax.axis_index("row") % side
    my_x = lax.axis_index("col") // cores
    my_core = lax.axis_index("col") % cores

    def pair(place, first, second):
        return first | (second << code_bits) | (place << (2 * code_bits))

    for place in range(2 * kinds * blocks):
        waiting[place] = -1
    for which in range(2 * kinds):
        waiting[2 * kinds * blocks + which] = 0

    def turn(slot, carry):
        target = row_ref[slot]
        source = col_ref[slot]
        column = lax.shift_right_logical(target, log(blocks_dev))
        away_x = (lax.shift_right_logical(column, log(cores)) - my_x) & (side - 1)
        beside = away_x & 1
        kind = jnp.where(beside == 1, 1, jnp.where(away_x == across_x, 0, 2))
        right = (away_x > across_x).astype(jnp.int32)
        place = right * blocks_dev + (target & (blocks_dev - 1))
        which = kinds * (1 - ((column & (cores - 1)) ^ my_core)) + kind
        owner = lax.shift_right_logical(source, log(picks))
        away_z = (lax.shift_right_logical(owner, log(side)) - my_z) & (side - 1)
        away_y = (owner - my_y) & (side - 1)
        pos = (away_z * side + away_y) * picks + (source & (picks - 1))
        code = slot | (pos << slot_bits)
        before = waiting[which * blocks + place]
        end = waiting[2 * kinds * blocks + which]
        plan_ref[which * entries + end] = pair(place, before, code)
        waiting[which * blocks + place] = jnp.where(before >= 0, -1, code)
        waiting[2 * kinds * blocks + which] = end + (before >= 0).astype(jnp.int32)
        return carry

    lax.fori_loop(0, count_ref[0, 0], turn, 0)
    for which in range(2 * kinds):
        end = waiting[2 * kinds * blocks + which]
        for place in range(places_of(which, blocks_dev)):
            before = waiting[which * blocks + place]
            plan_ref[which * entries + end] = pair(place, before, empty)
            end = end + (before >= 0).astype(jnp.int32)
        for extra in range(unroll):
            plan_ref[which * entries + end + extra] = pair(0, empty, empty)
        plan_ref[2 * kinds * entries + which] = end


def pack(half, *refs):
    first, second = refs[:side], refs[side : 2 * side]
    notes_from = refs[2 * side : 4 * side - 2]
    outs = refs[4 * side - 2 : 6 * side - 4]
    notes, sems = refs[6 * side - 4 :]
    rows = side * half
    copies = [
        pltpu.make_async_copy(
            source.at[rows : rows + note_rows, :lanes], notes.at[at], sems.at[at]
        )
        for at, source in enumerate(notes_from)
    ]
    for copy in copies:
        copy.start()
    for copy in copies:
        copy.wait()
    my_z = lax.axis_index("row") // side
    my_y = lax.axis_index("row") % side
    for away in range(1, side):
        for d in range(side):
            next_y = lax.rem(my_y + d, side)
            next_z = lax.rem(my_z + d, side)
            for j in range(picks):
                spot = spot_of(d, j, half)
                along_z = notes[away - 1, j, my_z * side + next_y].astype(jnp.int32)
                outs[away - 1][spot, :] = first[d][half_at(along_z, half), :]
                along_y = notes[side + away - 2, j, next_z * side + my_y].astype(jnp.int32)
                outs[side + away - 2][spot, :] = second[d][half_at(along_y, half), :]


def pack_group(first, second, notes, half):
    packed = jax.ShapeDtypeStruct((side * picks * half, span), jnp.float32)
    number = 2 * (side - 1)
    return pl.pallas_call(
        lambda *refs: pack(half, *refs),
        in_specs=[in_vmem] * (2 * side + number),
        out_specs=[in_vmem] * number,
        scratch_shapes=[
            pltpu.SMEM((number, note_rows, lanes), jnp.float32),
            pltpu.SemaphoreType.DMA((number,)),
        ],
        out_shape=[packed] * number,
        compiler_params=pltpu.CompilerParams(vmem_limit_bytes=5 << 20),
        cost_estimate=pl.CostEstimate(flops=0, bytes_accessed=5 << 20, transcendentals=0),
        name="pack",
    )(*first, *second, *notes)


def add_tiles(which, blocks_dev, plan_ref, tile_ref, pool, total):
    at_once = unroll if which % kinds == 1 else unroll // 2
    tile_total = tile_ref.shape[0]
    sources = pool.shape[0] - 1
    entries = pairs_of(tile_total, blocks_dev)
    slot_bits = log(tile_total)
    pos_bits = log(sources) + 1

    def turn(step, carry):
        products = []
        for lane in range(at_once):
            code = plan_ref[which * entries + step * at_once + lane]
            left, right = [], []
            for _ in range(2):
                left.append(tile_ref[code & (tile_total - 1)].astype(jnp.bfloat16))
                code = lax.shift_right_logical(code, slot_bits)
                right.append(pool[code & ((1 << pos_bits) - 1)])
                code = lax.shift_right_logical(code, pos_bits)
            product = jnp.dot(
                jnp.concatenate(left, axis=1),
                jnp.concatenate(right, axis=0),
                preferred_element_type=jnp.float32,
            )
            products.append((code, product))
        for target, product in products:
            total[target] += product
        return carry

    count = plan_ref[2 * kinds * entries + which]
    lax.fori_loop(0, (count + at_once - 1) // at_once, turn, 0)


def put(pool, along_z, along_y, away):
    half = pool.shape[1] // 2
    top, low = slice(0, half), slice(half, 2 * half)
    for d in range(side):
        for j in range(picks):
            spot = spot_of(d, j, half)
            pool[(back(away) * side + d) * picks + j, top, :] = along_z[spot, :].astype(pool.dtype)
            pool[(d * side + back(away)) * picks + j, low, :] = along_y[spot, :].astype(pool.dtype)


def fill(need_ref, *refs):
    first, second = refs[:side], refs[side : 2 * side]
    early, pool = refs[2 * side : -1], refs[-1]
    half = pool.shape[1] // 2
    top, low = slice(0, half), slice(half, 2 * half)
    my_z = lax.axis_index("row") // side
    my_y = lax.axis_index("row") % side
    for d in range(side):
        next_y = lax.rem(my_y + d, side)
        next_z = lax.rem(my_z + d, side)
        for j in range(picks):
            mine = need_ref[j, my_z * side + next_y]
            pool[d * picks + j, top, :] = first[d][half_at(mine, half), :].astype(pool.dtype)
            mine = need_ref[j, next_z * side + my_y]
            pool[d * side * picks + j, low, :] = second[d][half_at(mine, half), :].astype(
                pool.dtype
            )
    for at, away in enumerate(near):
        put(pool, early[2 * at], early[2 * at + 1], away)
    pool[side * side * picks] = jnp.zeros(pool.shape[1:], pool.dtype)


def fill_early(need, first, second, along_z, along_y, edge):
    early = [v for away in near for v in (along_z[away - 1], along_y[away - 1])]
    return pl.pallas_call(
        fill,
        in_specs=[in_smem] + [in_vmem] * (2 * side + len(early)),
        out_specs=in_vmem,
        out_shape=jax.ShapeDtypeStruct((side * side * picks + 1, edge, span), jnp.bfloat16),
        compiler_params=pltpu.CompilerParams(vmem_limit_bytes=8 << 20),
        cost_estimate=pl.CostEstimate(flops=0, bytes_accessed=5 << 20, transcendentals=0),
        name="fill",
    )(need, *first, *second, *early)


def combine(blocks_dev, plan_ref, tile_ref, along_z, along_y, _, total, pool, listed, sem):
    copy = pltpu.make_async_copy(plan_ref, listed, sem)
    copy.start()
    total[...] = jnp.zeros_like(total)
    put(pool, along_z, along_y, side // 2)
    copy.wait()
    add_tiles(0, blocks_dev, listed, tile_ref, pool, total)


def combine_sent(listed, tiles, along_z, along_y, pool, blocks_dev):
    edge = tiles.shape[1]
    far = side // 2 - 1
    return pl.pallas_call(
        lambda *refs: combine(blocks_dev, *refs),
        in_specs=[in_vmem] * 5,
        out_specs=[in_vmem] * 2,
        scratch_shapes=[pltpu.SMEM(listed.shape, jnp.int32), pltpu.SemaphoreType.DMA(())],
        out_shape=[
            jax.ShapeDtypeStruct((places_of(0, blocks_dev), edge, span), jnp.float32),
            jax.ShapeDtypeStruct(pool.shape, pool.dtype),
        ],
        input_output_aliases={4: 1},
        compiler_params=pltpu.CompilerParams(vmem_limit_bytes=10 << 20),
        cost_estimate=pl.CostEstimate(flops=2 << 30, bytes_accessed=6 << 20, transcendentals=0),
        name="combine",
    )(listed, tiles, along_z[far], along_y[far], pool)


def combine_listed(which_ones, listed, tiles, pool, blocks_dev):
    edge = tiles.shape[1]

    def body(plan_ref, tile_ref, pool_ref, *refs):
        totals, (lists, sem) = refs[:-2], refs[-2:]
        copy = pltpu.make_async_copy(plan_ref, lists, sem)
        copy.start()
        for total in totals:
            total[...] = jnp.zeros_like(total)
        copy.wait()
        for which, total in zip(which_ones, totals):
            add_tiles(which, blocks_dev, lists, tile_ref, pool_ref, total)

    return pl.pallas_call(
        body,
        in_specs=[in_vmem] * 3,
        out_specs=[in_vmem] * len(which_ones),
        scratch_shapes=[pltpu.SMEM(listed.shape, jnp.int32), pltpu.SemaphoreType.DMA(())],
        out_shape=[
            jax.ShapeDtypeStruct((places_of(which, blocks_dev), edge, span), jnp.float32)
            for which in which_ones
        ],
        compiler_params=pltpu.CompilerParams(vmem_limit_bytes=6 << 20),
        cost_estimate=pl.CostEstimate(flops=2 << 30, bytes_accessed=8 << 20, transcendentals=0),
        name="listed",
    )(listed, tiles, pool)


def mix(group, feature_ref, keep, arrived, from_right, from_left, left_held, right_held, piece):
    part = slice(group * span, (group + 1) * span)
    pieces = keep.shape[0] // lanes // 2
    shift = 0 if left_held.shape[0] > lanes else piece
    whole = slice(piece * lanes, (piece + 1) * lanes)
    own = slice((piece - shift) * lanes, (piece - shift + 1) * lanes)
    mixed = []
    for low, ready, held in ((0, from_right, left_held), (1, from_left, right_held)):
        spot = slice((low * pieces + piece) * lanes, (low * pieces + piece + 1) * lanes)
        summed = keep[spot, :] + arrived[spot, :] + ready[whole, :] + held[own, :]
        mixed.append(((1.0 + gin_epsilon) * feature_ref[spot, part] + summed).astype(jnp.bfloat16))
    return mixed


def begin_mlp(feature_ref, w_ref, bias_ref, *refs):
    totals, (out_ref, mixed) = refs[:-2], refs[-2:]
    for piece in range(mixed.shape[0] // lanes // 2):
        for low, value in enumerate(mix(0, feature_ref, *totals, piece)):
            mixed[(2 * piece + low) * lanes : (2 * piece + low + 1) * lanes, :] = value

    def turn(step, carry):
        part = pl.ds(pl.multiple_of(step * chunk, chunk), chunk)
        out_ref[part, :] = (
            jnp.dot(mixed[part, :], w_ref[:span, :], preferred_element_type=jnp.float32)
            + bias_ref[...]
        )
        return carry

    lax.fori_loop(0, out_ref.shape[0] // chunk, turn, 0)


def end_mlp(piece, feature_ref, w_ref, before_ref, w_out_ref, bias_ref, *refs):
    totals = refs[:6]
    if piece == 0:
        result, mixed = refs[6:]
    else:
        before_result, out_ref, mixed, result, sems = refs[6:]

        def move(source, at, low, columns):
            start = (low * out_ref.shape[0] // 2) + at * lanes
            copies.append(
                pltpu.make_async_copy(
                    source.at[low * lanes : (low + 1) * lanes, columns],
                    out_ref.at[start : start + lanes, columns],
                    sems.at[len(copies)],
                )
            )
            return copies[-1]

        copies = []
        for low in range(2):
            move(before_result, 0, low, slice(None))
        for copy in copies:
            copy.start()
    for low, value in enumerate(mix(1, feature_ref, *totals, piece)):
        mixed[low * lanes : (low + 1) * lanes, :] = value
    rows = mixed.shape[0]
    hidden = before_ref[piece * rows : (piece + 1) * rows, :] + jnp.dot(
        mixed[...], w_ref[span:, :], preferred_element_type=jnp.float32
    )
    hidden = jnp.maximum(hidden, 0.0).astype(jnp.bfloat16)
    for start in range(0, result.shape[1], span):
        columns = slice(start, start + span)
        updated = jnp.dot(hidden, w_out_ref[:, columns], preferred_element_type=jnp.float32)
        result[:, columns] = (updated + bias_ref[:, columns]).astype(result.dtype)
        for low in range(2 if piece else 0):
            move(result, 1, low, columns).start()
    for copy in copies if piece else []:
        copy.wait()


def on_device(
    features, tiles, tile_rows, tile_cols, tile_count, needed, w_in, bias_in, w_out, bias_out
):
    edge = tiles.shape[-1]
    half = edge // 2
    nodes, width = features.shape
    blocks_dev = nodes // edge
    hidden_size = w_in.shape[1]
    blocks = places_of(1, blocks_dev)
    groups = width // span

    need = needed[0, 0].T
    firsts, seconds = [], []
    for group in range(groups):
        top, low = split_group(group, features, need)
        first = [top] + [None] * (side - 1)
        second = [low] + [None] * (side - 1)
        for away in (1, 3, 2):
            first[away] = from_y(first[0], away)
            second[away] = from_z(second[0], away)
        firsts.append(first)
        seconds.append(second)
    notes = seconds[0][1:] + firsts[0][1:]

    listed = pl.pallas_call(
        lambda *refs: plan(*refs, blocks_dev),
        in_specs=[in_smem] * 3,
        out_specs=in_smem,
        out_shape=jax.ShapeDtypeStruct((512,), jnp.int32),
        scratch_shapes=[pltpu.SMEM((2 * kinds * (blocks + 1),), jnp.int32)],
        compiler_params=pltpu.CompilerParams(vmem_limit_bytes=1 << 20),
        cost_estimate=pl.CostEstimate(flops=0, bytes_accessed=1 << 20, transcendentals=0),
        name="plan",
    )(tile_rows[0, 0], tile_cols[0, 0], tile_count)
    cell_tiles = tiles[0, 0]

    sums = []
    for group in range(groups):
        first, second = firsts[group], seconds[group]
        packed = pack_group(first, second, notes, half)
        along_z, along_y = [None] * (side - 1), [None] * (side - 1)
        for away in (1, 3, 2):
            along_z[away - 1] = from_z(packed[away - 1], -away)
            along_y[away - 1] = from_y(packed[side + away - 2], -away)
        pool = fill_early(need, first, second, along_z, along_y, edge)
        send, pool = combine_sent(listed, cell_tiles, along_z, along_y, pool, blocks_dev)
        arrived = lax.ppermute(send, "col", col_shift(0, 1))
        keep, sides = combine_listed((kinds, 1), listed, cell_tiles, pool, blocks_dev)
        over_right, over_left = pl.pallas_call(
            join_across,
            in_specs=[in_vmem] * 2,
            out_specs=[in_vmem] * 2,
            out_shape=[jax.ShapeDtypeStruct((blocks_dev // 2, edge, span), jnp.float32)] * 2,
            compiler_params=pltpu.CompilerParams(vmem_limit_bytes=4 << 20),
            cost_estimate=pl.CostEstimate(flops=0, bytes_accessed=2 << 20, transcendentals=0),
            name="join",
        )(keep, arrived)
        relay_right = lax.ppermute(over_right, "col", col_shift(1, 0))
        relay_left = lax.ppermute(over_left, "col", col_shift(-1, 0))
        arrived = lax.ppermute(sides, "col", col_shift(0, 1))
        keep, mine_sent, mine_kept = combine_listed(
            (kinds + 1, 2, kinds + 2), listed, cell_tiles, pool, blocks_dev
        )
        cut = blocks_dev // 2
        held = [cut] if group < groups - 1 else [1] * cut
        sizes = held + [cut, cut] + held
        joined = pl.pallas_call(
            join_rest,
            in_specs=[in_vmem] * 2,
            out_specs=[in_vmem] * len(sizes),
            out_shape=[jax.ShapeDtypeStruct((n, edge, span), jnp.float32) for n in sizes],
            compiler_params=pltpu.CompilerParams(vmem_limit_bytes=6 << 20),
            cost_estimate=pl.CostEstimate(flops=0, bytes_accessed=4 << 20, transcendentals=0),
            name="join",
        )(keep, arrived)
        right_held, (right, left) = joined[: len(held)], joined[len(held) : len(held) + 2]
        left_held = joined[len(held) + 2 :]
        from_left = lax.ppermute(right, "col", col_shift(1, 0))
        from_right = lax.ppermute(left, "col", col_shift(-1, 0))
        relayed = pl.pallas_call(
            relay,
            in_specs=[in_vmem] * (2 + 2 * len(held)),
            out_specs=[in_vmem] * (2 * len(held)),
            out_shape=[jax.ShapeDtypeStruct((n, edge, span), jnp.float32) for n in held * 2],
            compiler_params=pltpu.CompilerParams(vmem_limit_bytes=4 << 20),
            cost_estimate=pl.CostEstimate(flops=0, bytes_accessed=2 << 20, transcendentals=0),
            name="relay",
        )(relay_right, relay_left, *right_held, *left_held)
        from_left_held, from_right_held = [], []
        for piece in range(len(held)):
            from_left_held.append(
                lax.ppermute(relayed[piece], "col", col_shift(1, 0))
            )
            from_right_held.append(
                lax.ppermute(relayed[len(held) + piece], "col", col_shift(-1, 0))
            )
        arrived = lax.ppermute(mine_sent, "col", col_shift(0, 1))
        sums.append((mine_kept, arrived, from_right, from_left, from_left_held, from_right_held))

    flat = [[jax.tree.map(lambda v: v.reshape(-1, span), part) for part in one] for one in sums]
    *ready, (left_part,), (right_part,) = flat[0]
    before = pl.pallas_call(
        begin_mlp,
        in_specs=[in_vmem] * 9,
        out_specs=in_vmem,
        out_shape=jax.ShapeDtypeStruct((nodes, hidden_size), jnp.float32),
        scratch_shapes=[pltpu.VMEM((nodes, span), jnp.bfloat16)],
        compiler_params=pltpu.CompilerParams(vmem_limit_bytes=8 << 20),
        cost_estimate=pl.CostEstimate(
            flops=1 << 29, bytes_accessed=8 << 20, transcendentals=0
        ),
        name="begin",
    )(features, w_in, bias_in.reshape(1, -1), *ready, left_part, right_part)
    updated = []
    *ready, left_parts, right_parts = flat[1]
    for piece in range(len(left_parts)):
        rows = nodes // len(left_parts)
        last = piece == len(left_parts) - 1
        updated = [
            pl.pallas_call(
                lambda *refs: end_mlp(piece, *refs),
                in_specs=[in_vmem] * (11 + len(updated)),
                out_specs=pl.BlockSpec(memory_space=pltpu.HBM) if last else in_vmem,
                out_shape=jax.ShapeDtypeStruct((nodes if last else rows, width), jnp.bfloat16),
                scratch_shapes=[pltpu.VMEM((rows, span), jnp.bfloat16)]
                + (
                    [pltpu.VMEM((rows, width), jnp.bfloat16), pltpu.SemaphoreType.DMA((6,))]
                    if last
                    else []
                ),
                compiler_params=pltpu.CompilerParams(vmem_limit_bytes=8 << 20),
                cost_estimate=pl.CostEstimate(
                    flops=3 << 28, bytes_accessed=4 << 20, transcendentals=0
                ),
                name="end",
            )(
                features,
                w_in,
                before,
                w_out,
                bias_out.reshape(1, -1),
                *ready,
                left_parts[piece],
                right_parts[piece],
                *updated,
            )
        ]
    return updated[0]


def solution(mesh):
    placed = (
        P(("row", "col"), None),
        P("row", "col", None, None, None),
        P("row", "col", None),
        P("row", "col", None),
        P("row", "col"),
        P("row", "col", None, None),
        P(),
        P(),
        P(),
        P(),
    )

    return jax.shard_map(
        on_device, mesh=mesh, in_specs=placed, out_specs=P(("row", "col"), None), check_vma=False
    )
```
